32 devices in a mesh: groups: 2 (over y), seq: 4 (over z), mp: 4 (over x, core).
Axes of the slice: x: 2, y: 2, z: 4, core: 2. Of those that a mesh axis runs over, the one named last changes fastest.
Arguments:
- node_vectors: bfloat16 [1024, 2048], P(('groups', 'seq'), 'mp'), parts along dimension 0, may hold values from -6 to 6
- standardize_multiplier: float32 [2048], replicated, may hold values from 0.1 to 1.9
- probe_matrix: bfloat16 [2048, 1024], P(None, 'mp'), may hold values from -1 to 1
- lookup_matrix: bfloat16 [2048, 1024], P(None, 'mp'), may hold values from -1 to 1
- content_matrix: bfloat16 [2048, 1024], P(None, 'mp'), may hold values from -0.125 to 0.125
- softness_per_group: float32 [8], P('mp'), may hold values from 0.5 to 12
- exit_matrix: bfloat16 [1024, 2048], P('mp'), may hold values from -0.1875 to 0.1875
Outputs:
- mixed: bfloat16 [1024, 2048], P(('groups', 'seq'), 'mp'), parts along dimension 0
The draws below stay inside these ranges and needn't reach their ends.
There are 2 independent parts, one for each index of `groups`. The reference program is written for one: setup_inputs(seed, part) draws one part's arguments, and reference() takes and returns one part's arrays. A program takes and returns all parts, laid end to end along the dimension named above; an argument that names none is the same for every part. Nothing has to cross between parts.
All inputs are finite; a program needn't handle non-finite values.
Results may differ from the reference program's by a relative error of at most 0.011.
Values may be sent and summed in bfloat16 or wider, within the bound.
A program may use at most 64 MiB of HBM per device.

```python
import math
import jax
import jax.numpy as jnp
from jax import lax

D = 2048
HEADS = 8
CHANNEL_SPAN = 128
LENGTH = 512


def draw_node_vectors(key, part):
    drawn = jax.random.normal(jax.random.fold_in(key, 21), (LENGTH, D), jnp.float32)
    return jnp.clip(drawn, -6.0, 6.0).astype(jnp.bfloat16)


def query_matrix(key):
    return jax.random.normal(jax.random.fold_in(key, 31), (D, HEADS * CHANNEL_SPAN), jnp.float32) / math.sqrt(D)


def draw_probe_matrix(key, part):
    return jnp.clip(query_matrix(key), -1.0, 1.0).astype(jnp.bfloat16)


def draw_lookup_matrix(key, part):
    drawn = jax.random.normal(jax.random.fold_in(key, 32), (D, HEADS * CHANNEL_SPAN), jnp.float32) / math.sqrt(D)
    return jnp.clip(drawn, -1.0, 1.0).astype(jnp.bfloat16)


def draw_softness_per_group(key, part):
    uniform_draw = jax.random.uniform(jax.random.fold_in(key, 41), (HEADS,), jnp.float32)
    return jnp.power(4.0, uniform_draw)


def block_scale(own_key, dims, shards, smallest, top_value):
    loudness = 1.0
    for dim, parts in shards:
        steps = jax.random.uniform(jax.random.fold_in(jax.random.fold_in(own_key, 6), dim), (parts,), jnp.float32, smallest / len(shards), top_value / len(shards))
        loudness = loudness * jnp.repeat(jnp.exp(steps), dims[dim] // parts).reshape((-1,) + (1,) * (len(dims) - 1 - dim))
    return loudness


def scatter_about(stream_key, shape, width, most, cuts=(), dtype=jnp.bfloat16):
    entries = jax.random.normal(stream_key, shape, jnp.float32) * width
    if len(cuts) > 0:
        entries = block_scale(stream_key, shape, cuts, -0.22, 0.18) * entries
    return jnp.clip(entries, min=-most, max=most).astype(dtype)


def setup_inputs(seed: int = 0, part: int = 0) -> dict:
    key_list = jax.random.split(jax.random.key(seed), 8)
    own_keys = jax.random.split(jax.random.fold_in(key_list[7], part), 8)
    node_vectors = draw_node_vectors(jax.random.fold_in(jax.random.fold_in(key_list[7], part), 71), part)
    standardize_multiplier = jnp.clip(1.0 + 0.18 * jax.random.normal(key_list[1], (D,), jnp.float32), 0.1, 1.9)
    probe_matrix = draw_probe_matrix(jax.random.fold_in(key_list[7], 71), part)
    lookup_matrix = draw_lookup_matrix(jax.random.fold_in(key_list[7], 71), part)
    content_matrix = scatter_about(key_list[4], (D, HEADS * CHANNEL_SPAN), D ** -0.5, 0.125, ((1, 4),))
    softness_per_group = draw_softness_per_group(jax.random.fold_in(key_list[7], 71), part)
    exit_matrix = scatter_about(key_list[6], (HEADS * CHANNEL_SPAN, D), (HEADS * CHANNEL_SPAN) ** -0.5, 0.1875, ((0, 4),))
    return dict(node_vectors=node_vectors, standardize_multiplier=standardize_multiplier, probe_matrix=probe_matrix, lookup_matrix=lookup_matrix, content_matrix=content_matrix, softness_per_group=softness_per_group, exit_matrix=exit_matrix)


def reference(node_vectors, standardize_multiplier, probe_matrix, lookup_matrix, content_matrix, softness_per_group, exit_matrix):
    widened = node_vectors.astype(jnp.float32)
    average = lax.optimization_barrier(jnp.mean(widened, axis=-1, keepdims=True))
    centered = widened - average
    variance = lax.optimization_barrier(jnp.mean(centered * centered, axis=-1, keepdims=True))
    normed = (centered * lax.rsqrt(variance + 1e-05) * standardize_multiplier).astype(jnp.bfloat16)
    queries = jnp.dot(normed, probe_matrix, preferred_element_type=jnp.float32).astype(jnp.bfloat16)
    key_rows = jnp.dot(normed, lookup_matrix, preferred_element_type=jnp.float32).astype(jnp.bfloat16)
    value_rows = jnp.dot(normed, content_matrix, preferred_element_type=jnp.float32).astype(jnp.bfloat16)
    query_heads = queries.reshape(LENGTH, HEADS, CHANNEL_SPAN).transpose(1, 0, 2)
    key_heads = key_rows.reshape(LENGTH, HEADS, CHANNEL_SPAN).transpose(1, 0, 2)
    value_heads = value_rows.reshape(LENGTH, HEADS, CHANNEL_SPAN).transpose(1, 0, 2)
    inverse_root_span = softness_per_group / math.sqrt(CHANNEL_SPAN)
    block_rows = math.gcd(LENGTH, 1024)

    def one_head(inputs):
        head_queries, head_keys, head_values, head_factor = inputs

        def one_block(query_block):
            scores = jnp.dot(query_block, head_keys.T, preferred_element_type=jnp.float32) * head_factor
            row_max = lax.optimization_barrier(jnp.max(scores, axis=-1, keepdims=True))
            weights = jnp.exp(scores - row_max)
            totals = lax.optimization_barrier(jnp.sum(weights, axis=-1, keepdims=True))
            attended = jnp.dot(weights.astype(jnp.bfloat16), head_values, preferred_element_type=jnp.float32)
            return attended / totals
        blocks = head_queries.reshape(LENGTH // block_rows, block_rows, CHANNEL_SPAN)
        return lax.map(one_block, blocks).reshape(LENGTH, CHANNEL_SPAN)
    attended = lax.map(one_head, (query_heads, key_heads, value_heads, inverse_root_span))
    heads_out = attended.transpose(1, 0, 2).reshape(LENGTH, HEADS * CHANNEL_SPAN).astype(jnp.bfloat16)
    projected = jnp.dot(heads_out, exit_matrix, preferred_element_type=jnp.float32)
    return (widened + projected).astype(jnp.bfloat16)
```

```python
import functools
import math

import jax
import jax.numpy as jnp
from jax import lax
from jax.experimental import pallas as pl
from jax.experimental.pallas import tpu as pltpu
from jax.sharding import PartitionSpec as P

MESH = pl.DeviceIdType.MESH
F32 = jnp.float32
BF16 = jnp.bfloat16
UNROLL_LIMIT = 8
RS_PIECES = 2


def remote(src, dst, send_sem, recv_sem, axis, index):
    return pltpu.make_async_remote_copy(
        src_ref=src,
        dst_ref=dst,
        send_sem=send_sem,
        recv_sem=recv_sem,
        device_id={axis: index},
        device_id_type=MESH,
    )


def each(count, body):
    if count <= UNROLL_LIMIT:
        for i in range(count):
            body(i)
    else:
        lax.fori_loop(0, count, lambda i, c: (body(i), c)[1], 0)


def kernel(
    n_mp,
    n_seq,
    softness_hbm,
    x_hbm,
    gain_hbm,
    wq_hbm,
    wk_hbm,
    wv_hbm,
    wo_hbm,
    out_ref,
    softness_ref,
    gain_ref,
    xg,
    wq,
    wk,
    wv,
    wo,
    normed,
    q_ref,
    kv,
    scores,
    heads,
    out_send,
    out_recv,
    small_sem,
    w_sem,
    x_sem,
    xg_send,
    xg_recv,
    kv_send,
    kv_recv,
    rs_send,
    rs_recv,
):
    me = lax.axis_index("mp")
    spot = lax.axis_index("seq")
    rows, part = x_hbm.shape
    head_cols = wq_hbm.shape[1]
    groups = softness_hbm.shape[0]
    span = head_cols // groups
    paired = n_mp == 4
    has_left = spot > 0
    has_right = spot < n_seq - 1
    hop = n_seq == 4
    ends = (spot == 0) | (spot == n_seq - 1)

    own_x = pltpu.make_async_copy(x_hbm, xg.at[me], x_sem)
    own_x.start()
    smalls = [
        pltpu.make_async_copy(gain_hbm, gain_ref, small_sem.at[0]),
        pltpu.make_async_copy(softness_hbm, softness_ref, small_sem.at[1]),
    ]
    for small in smalls:
        small.start()
    loads = [
        pltpu.make_async_copy(src, dst, w_sem.at[i])
        for i, (src, dst) in enumerate(((wk_hbm, wk), (wv_hbm, wv), (wq_hbm, wq), (wo_hbm, wo)))
    ]
    for load in loads:
        load.start()

    barrier = pltpu.get_barrier_semaphore()
    for step in range(1, n_mp):
        pl.semaphore_signal(
            barrier, inc=1, device_id={"mp": lax.rem(me + step, n_mp)}, device_id_type=MESH
        )

    @pl.when(has_left)
    def _():
        pl.semaphore_signal(barrier, inc=1, device_id={"seq": spot - 1}, device_id_type=MESH)

    @pl.when(has_right)
    def _():
        pl.semaphore_signal(barrier, inc=1, device_id={"seq": spot + 1}, device_id_type=MESH)

    greeted = n_mp - 1 + has_left.astype(jnp.int32) + has_right.astype(jnp.int32)
    if hop:

        @pl.when(ends)
        def _():
            pl.semaphore_signal(
                barrier, inc=1, device_id={"seq": n_seq - 1 - spot}, device_id_type=MESH
            )

        greeted = greeted + ends.astype(jnp.int32)
    pl.semaphore_wait(barrier, greeted)

    half = rows // 2
    pieces = [pl.ds(0, half), pl.ds(half, half)]
    near = me + 1 - 2 * lax.rem(me, 2)
    far = lax.rem(me + 2, n_mp)
    cross = lax.rem(near + 2, n_mp)
    sends = []

    def gather(lane, c, source, target):
        slot = xg.at[source, pieces[c]]
        return remote(slot, slot, xg_send.at[lane, c], xg_recv.at[lane, c], "mp", target)

    if paired:
        for lane, peer in ((0, far), (1, near)):
            for c, piece in enumerate(pieces):
                send = remote(
                    x_hbm.at[piece], xg.at[me, piece],
                    xg_send.at[lane, c], xg_recv.at[lane, c], "mp", peer,
                )
                send.start()
                sends.append(send)
    else:
        for c, piece in enumerate(pieces):
            for step in range(1, n_mp):
                send = remote(
                    x_hbm.at[piece], xg.at[me, piece],
                    xg_send.at[step, c], xg_recv.at[step, c], "mp", lax.rem(me + step, n_mp),
                )
                send.start()
                sends.append(send)
    own_x.wait()
    for small in smalls:
        small.wait()

    def relay_far(c):
        if paired:
            gather(0, c, far, far).wait_recv()
            relay = gather(2, c, far, near)
            relay.start()
            sends.append(relay)

    def gathered(c):
        if paired:
            gather(1, c, near, near).wait_recv()
            gather(2, c, cross, near).wait_recv()
        else:
            for step in range(1, n_mp):
                source = lax.rem(me - step + n_mp, n_mp)
                gather(step, c, source, source).wait_recv()

    features = n_mp * part

    def normalize(c):
        piece = pieces[c]
        total = jnp.zeros((half, 1), F32)
        for j in range(n_mp):
            total = total + jnp.sum(xg[j, piece, :].astype(F32), axis=-1, keepdims=True)
        average = total / features
        square = jnp.zeros((half, 1), F32)
        for j in range(n_mp):
            off = xg[j, piece, :].astype(F32) - average
            square = square + jnp.sum(off * off, axis=-1, keepdims=True)
        inverse = lax.rsqrt(square / features + 1e-05)
        for j in range(n_mp):
            cols = pl.ds(j * part, part)
            off = xg[j, piece, :].astype(F32) - average
            normed[piece, cols] = (off * inverse * gain_ref[:, cols]).astype(BF16)

    def block(way, which, owner, c, target):
        slot = kv.at[which, owner, pieces[c]]
        return remote(
            slot, slot, kv_send.at[way, which, owner, c], kv_recv.at[which, owner, c], "seq", target
        )

    def project(which, weight, c):
        kv[which, spot, pieces[c]] = jnp.dot(
            normed[pieces[c], :], weight[...], preferred_element_type=F32
        ).astype(BF16)
        launch(which, c)

    def launch(which, c):
        @pl.when(has_right)
        def _():
            block(1, which, spot, c, spot + 1).start()

        @pl.when(has_left)
        def _():
            block(0, which, spot, c, spot - 1).start()

        if hop:

            @pl.when(ends)
            def _():
                block(2, which, spot, c, n_seq - 1 - spot).start()

    relay_far(0)
    gathered(0)
    normalize(0)
    relay_far(1)
    loads[0].wait()
    project(0, wk, 0)
    gathered(1)
    normalize(1)
    project(0, wk, 1)
    loads[1].wait()
    kv[1, spot] = jnp.dot(normed[...], wv[...], preferred_element_type=F32).astype(BF16)
    for c in range(2):
        launch(1, c)
    loads[2].wait()
    q_ref[...] = jnp.dot(normed[...], wq[...], preferred_element_type=F32).astype(BF16)

    def take(which, step, c, forward):
        before = spot - step
        after = spot + step

        @pl.when(before >= 0)
        def _():
            block(1, which, before, c, before).wait_recv()
            if forward:

                @pl.when(has_right)
                def _():
                    block(1, which, before, c, spot + 1).start()

        @pl.when(after < n_seq)
        def _():
            block(0, which, after, c, after).wait_recv()
            if forward:

                @pl.when(has_left)
                def _():
                    block(0, which, after, c, spot - 1).start()

    if hop:
        for which in range(2):
            for c in range(2):
                take(which, 1, c, True)
        for step in (2, 3):
            for c in range(2):
                take(0, step, c, False)

        def last_values():
            for step in (2, 3):
                for c in range(2):
                    take(1, step, c, False)

    else:

        def chain(i):
            for c in range(2):
                for which in range(2):
                    take(which, i + 1, c, True)

        each(n_seq - 1, chain)

        def last_values():
            pass

    if n_seq <= UNROLL_LIMIT:
        sums, chances = [], []
        for h in range(groups):
            cols = pl.ds(h * span, span)
            keys = kv[0, :, :, cols].reshape(n_seq * rows, span)
            s = lax.dot_general(
                q_ref[:, cols], keys, (((1,), (1,)), ((), ())), preferred_element_type=F32
            ) * (softness_ref[h] / math.sqrt(span))
            top = jnp.max(s, axis=-1, keepdims=True)
            w = jnp.exp(s - top)
            sums.append(jnp.sum(w, axis=-1, keepdims=True))
            chances.append(w.astype(BF16))
        last_values()
        for h in range(groups):
            cols = pl.ds(h * span, span)
            values = kv[1, :, :, cols].reshape(n_seq * rows, span)
            mixed = jnp.dot(chances[h], values, preferred_element_type=F32)
            heads[:, cols] = (mixed / sums[h]).astype(BF16)
    else:
        for h in range(groups):
            cols = pl.ds(h * span, span)
            factor = softness_ref[h] / math.sqrt(span)

            def first(b, top):
                s = lax.dot_general(
                    q_ref[:, cols], kv[0, b, :, cols], (((1,), (1,)), ((), ())),
                    preferred_element_type=F32,
                ) * factor
                scores[b] = s
                return jnp.maximum(top, jnp.max(s, axis=-1, keepdims=True))

            top = lax.fori_loop(0, n_seq, first, jnp.full((rows, 1), -jnp.inf, F32))

            def second(b, state):
                summed, mixed = state
                w = jnp.exp(scores[b] - top)
                mixed = mixed + jnp.dot(
                    w.astype(BF16), kv[1, b, :, cols], preferred_element_type=F32
                )
                return summed + jnp.sum(w, axis=-1, keepdims=True), mixed

            summed, mixed = lax.fori_loop(
                0, n_seq, second, (jnp.zeros((rows, 1), F32), jnp.zeros((rows, span), F32))
            )
            heads[:, cols] = (mixed / summed).astype(BF16)

    loads[3].wait()
    rs_pieces = [pl.ds(i * (rows // RS_PIECES), rows // RS_PIECES) for i in range(RS_PIECES)]

    def share(owner):
        cols = pl.ds(pl.multiple_of(owner * part, part), part)
        return jnp.dot(heads[...], wo[:, cols], preferred_element_type=F32)

    if paired:
        quarter = rows // len(rs_pieces)

        def reduce(lane, piece, target):
            return remote(
                out_send.at[lane, piece], out_recv.at[lane, piece],
                rs_send.at[lane, piece.start // quarter], rs_recv.at[lane, piece.start // quarter],
                "mp", target,
            )

        out_send[0] = share(cross).astype(BF16)
        for piece in rs_pieces:
            send = reduce(0, piece, near)
            send.start()
            sends.append(send)
        for_far = share(far)
        for piece in rs_pieces:
            reduce(0, piece, near).wait_recv()
            low = piece.start
            out_send[2, piece] = (
                for_far[low : low + quarter] + out_recv[0, piece].astype(F32)
            ).astype(BF16)
            send = reduce(2, piece, far)
            send.start()
            sends.append(send)
        out_send[1] = share(near).astype(BF16)
        for piece in rs_pieces:
            send = reduce(1, piece, near)
            send.start()
            sends.append(send)
        own = share(me) + xg[me].astype(F32)
        for piece in rs_pieces:
            reduce(1, piece, near).wait_recv()
        own = own + out_recv[1].astype(F32)
        for piece in rs_pieces:
            reduce(2, piece, far).wait_recv()
            low = piece.start
            out_ref[piece, :] = (
                own[low : low + quarter] + out_recv[2, piece].astype(F32)
            ).astype(BF16)
    else:
        for step in range(1, n_mp):
            peer = lax.rem(me + step, n_mp)
            out_send[step] = share(peer).astype(BF16)
            send = remote(
                out_send.at[step], out_recv.at[step], rs_send.at[step, 0], rs_recv.at[step, 0], "mp", peer
            )
            send.start()
            sends.append(send)
        own = share(me) + xg[me].astype(F32)
        for step in range(1, n_mp):
            remote(
                out_send.at[step], out_recv.at[step], rs_send.at[step, 0], rs_recv.at[step, 0], "mp", me
            ).wait_recv()
            own = own + out_recv[step].astype(F32)
        out_ref[...] = own.astype(BF16)

    for send in sends:
        send.wait_send()

    def drain(b):
        for which in range(2):
            for c in range(2):
                to_right = (b == spot) | (b == spot - 1) if hop else b <= spot
                to_left = (b == spot) | (b == spot + 1) if hop else b >= spot

                @pl.when(has_right & to_right)
                def _():
                    block(1, which, b, c, spot + 1).wait_send()

                @pl.when(has_left & to_left)
                def _():
                    block(0, which, b, c, spot - 1).wait_send()

                if hop:

                    @pl.when(ends & (b == spot))
                    def _():
                        block(2, which, b, c, n_seq - 1 - spot).wait_send()

    each(n_seq, drain)


def per_device(n_mp, n_seq, x, gain, wq, wk, wv, softness, wo):
    rows, part = x.shape
    features, head_cols = wq.shape
    span_rows = n_seq if n_seq > UNROLL_LIMIT else 1
    any_space = pl.BlockSpec(memory_space=pl.ANY)
    vmem = pl.BlockSpec(memory_space=pltpu.VMEM)
    slots = max(n_mp, 3)
    return pl.pallas_call(
        functools.partial(kernel, n_mp, n_seq),
        out_shape=pltpu.VMEM((rows, part), BF16),
        in_specs=[
            any_space, any_space, any_space, any_space, any_space, any_space, any_space,
        ],
        out_specs=vmem,
        scratch_shapes=[
            pltpu.SMEM(softness.shape, F32),
            pltpu.VMEM((1, features), F32),
            pltpu.VMEM((n_mp, rows, part), BF16),
            pltpu.VMEM((features, head_cols), BF16),
            pltpu.VMEM((features, head_cols), BF16),
            pltpu.VMEM((features, head_cols), BF16),
            pltpu.VMEM((head_cols, features), BF16),
            pltpu.VMEM((rows, features), BF16),
            pltpu.VMEM((rows, head_cols), BF16),
            pltpu.VMEM((2, n_seq, rows, head_cols), BF16),
            pltpu.VMEM((span_rows, rows, rows), F32),
            pltpu.VMEM((rows, head_cols), BF16),
            pltpu.VMEM((slots, rows, part), BF16),
            pltpu.VMEM((slots, rows, part), BF16),
            pltpu.SemaphoreType.DMA((2,)),
            pltpu.SemaphoreType.DMA((4,)),
            pltpu.SemaphoreType.DMA,
            pltpu.SemaphoreType.DMA((slots, 2)),
            pltpu.SemaphoreType.DMA((slots, 2)),
            pltpu.SemaphoreType.DMA((3, 2, n_seq, 2)),
            pltpu.SemaphoreType.DMA((2, n_seq, 2)),
            pltpu.SemaphoreType.DMA((slots, RS_PIECES)),
            pltpu.SemaphoreType.DMA((slots, RS_PIECES)),
        ],
        compiler_params=pltpu.CompilerParams(collective_id=0, has_side_effects=True),
    )(softness, x, gain.reshape(1, features), wq, wk, wv, wo)


def solution(mesh):
    return jax.shard_map(
        functools.partial(per_device, mesh.shape["mp"], mesh.shape["seq"]),
        mesh=mesh,
        in_specs=(
            P(("groups", "seq"), "mp"),
            P(),
            P(None, "mp"),
            P(None, "mp"),
            P(None, "mp"),
            P("mp"),
            P("mp", None),
        ),
        out_specs=P(("groups", "seq"), "mp"),
        check_vma=False,
    )
```

```python
import functools
import math

import jax
import jax.numpy as jnp
from jax import lax
from jax.experimental import pallas as pl
from jax.experimental.pallas import tpu as pltpu
from jax.sharding import PartitionSpec as P

MESH = pl.DeviceIdType.MESH
F32 = jnp.float32
BF16 = jnp.bfloat16
UNROLL_LIMIT = 8
RS_PIECES = 2
X_PIECES = 4
VMEM_BYTES = 60 * 1024 * 1024


def remote(src, dst, send_sem, recv_sem, axis, index):
    return pltpu.make_async_remote_copy(
        src_ref=src,
        dst_ref=dst,
        send_sem=send_sem,
        recv_sem=recv_sem,
        device_id={axis: index},
        device_id_type=MESH,
    )


def each(count, body):
    if count <= UNROLL_LIMIT:
        for i in range(count):
            body(i)
    else:
        lax.fori_loop(0, count, lambda i, c: (body(i), c)[1], 0)


def kernel(
    n_mp,
    n_seq,
    softness_hbm,
    x_hbm,
    gain_hbm,
    wq_hbm,
    wk_hbm,
    wv_hbm,
    wo_hbm,
    out_ref,
    softness_ref,
    gain_ref,
    xg,
    wq,
    wk,
    wv,
    wo,
    normed,
    q_ref,
    kv,
    scores,
    heads,
    out_send,
    out_recv,
    small_sem,
    w_sem,
    x_sem,
    xg_send,
    xg_recv,
    kv_send,
    kv_recv,
    rs_send,
    rs_recv,
):
    me = lax.axis_index("mp")
    spot = lax.axis_index("seq")
    rows, part = x_hbm.shape
    head_cols = wq_hbm.shape[1]
    groups = softness_hbm.shape[0]
    span = head_cols // groups
    paired = n_mp == 4
    has_left = spot > 0
    has_right = spot < n_seq - 1
    hop = n_seq == 4
    ends = (spot == 0) | (spot == n_seq - 1)

    own_x = pltpu.make_async_copy(x_hbm, xg.at[me], x_sem)
    own_x.start()
    smalls = [
        pltpu.make_async_copy(gain_hbm, gain_ref, small_sem.at[0]),
        pltpu.make_async_copy(softness_hbm, softness_ref, small_sem.at[1]),
    ]
    for small in smalls:
        small.start()
    loads = [
        pltpu.make_async_copy(src, dst, w_sem.at[i])
        for i, (src, dst) in enumerate(((wk_hbm, wk), (wv_hbm, wv), (wq_hbm, wq), (wo_hbm, wo)))
    ]
    for load in loads:
        load.start()

    barrier = pltpu.get_barrier_semaphore()
    for step in range(1, n_mp):
        pl.semaphore_signal(
            barrier, inc=1, device_id={"mp": lax.rem(me + step, n_mp)}, device_id_type=MESH
        )

    @pl.when(has_left)
    def _():
        pl.semaphore_signal(barrier, inc=1, device_id={"seq": spot - 1}, device_id_type=MESH)

    @pl.when(has_right)
    def _():
        pl.semaphore_signal(barrier, inc=1, device_id={"seq": spot + 1}, device_id_type=MESH)

    greeted = n_mp - 1 + has_left.astype(jnp.int32) + has_right.astype(jnp.int32)
    if hop:

        @pl.when(ends)
        def _():
            pl.semaphore_signal(
                barrier, inc=1, device_id={"seq": n_seq - 1 - spot}, device_id_type=MESH
            )

        greeted = greeted + ends.astype(jnp.int32)
    pl.semaphore_wait(barrier, greeted)

    half = rows // 2
    pieces = [pl.ds(0, half), pl.ds(half, half)]
    near = me + 1 - 2 * lax.rem(me, 2)
    far = lax.rem(me + 2, n_mp)
    cross = lax.rem(near + 2, n_mp)
    sends = []

    def gather(lane, c, source, target):
        slot = xg.at[source, pieces[c]]
        return remote(slot, slot, xg_send.at[lane, c], xg_recv.at[lane, c], "mp", target)

    if paired:
        for lane, peer in ((0, far), (1, near)):
            for c, piece in enumerate(pieces):
                send = remote(
                    x_hbm.at[piece], xg.at[me, piece],
                    xg_send.at[lane, c], xg_recv.at[lane, c], "mp", peer,
                )
                send.start()
                sends.append(send)
    else:
        for c, piece in enumerate(pieces):
            for step in range(1, n_mp):
                send = remote(
                    x_hbm.at[piece], xg.at[me, piece],
                    xg_send.at[step, c], xg_recv.at[step, c], "mp", lax.rem(me + step, n_mp),
                )
                send.start()
                sends.append(send)
    own_x.wait()
    for small in smalls:
        small.wait()

    def relay_far(c):
        if paired:
            gather(0, c, far, far).wait_recv()
            relay = gather(2, c, far, near)
            relay.start()
            sends.append(relay)

    def gathered(c):
        if paired:
            gather(1, c, near, near).wait_recv()
            gather(2, c, cross, near).wait_recv()
        else:
            for step in range(1, n_mp):
                source = lax.rem(me - step + n_mp, n_mp)
                gather(step, c, source, source).wait_recv()

    features = n_mp * part

    def normalize(c):
        piece = pieces[c]
        total = jnp.zeros((half, 1), F32)
        for j in range(n_mp):
            total = total + jnp.sum(xg[j, piece, :].astype(F32), axis=-1, keepdims=True)
        average = total / features
        square = jnp.zeros((half, 1), F32)
        for j in range(n_mp):
            off = xg[j, piece, :].astype(F32) - average
            square = square + jnp.sum(off * off, axis=-1, keepdims=True)
        inverse = lax.rsqrt(square / features + 1e-05)
        for j in range(n_mp):
            cols = pl.ds(j * part, part)
            off = xg[j, piece, :].astype(F32) - average
            normed[piece, cols] = (off * inverse * gain_ref[:, cols]).astype(BF16)

    def block(way, which, owner, c, target):
        slot = kv.at[which, owner, pieces[c]]
        return remote(
            slot, slot, kv_send.at[way, which, owner, c], kv_recv.at[which, owner, c], "seq", target
        )

    def project(which, weight, c):
        kv[which, spot, pieces[c]] = jnp.dot(
            normed[pieces[c], :], weight[...], preferred_element_type=F32
        ).astype(BF16)
        launch(which, c)

    def launch(which, c):
        @pl.when(has_right)
        def _():
            block(1, which, spot, c, spot + 1).start()

        @pl.when(has_left)
        def _():
            block(0, which, spot, c, spot - 1).start()

        if hop:

            @pl.when(ends)
            def _():
                block(2, which, spot, c, n_seq - 1 - spot).start()

    relay_far(0)
    gathered(0)
    normalize(0)
    relay_far(1)
    loads[0].wait()
    project(0, wk, 0)
    gathered(1)
    normalize(1)
    project(0, wk, 1)
    loads[1].wait()
    kv[1, spot] = jnp.dot(normed[...], wv[...], preferred_element_type=F32).astype(BF16)
    for c in range(2):
        launch(1, c)
    loads[2].wait()
    q_ref[...] = jnp.dot(normed[...], wq[...], preferred_element_type=F32).astype(BF16)

    def take(which, step, c, forward):
        before = spot - step
        after = spot + step

        @pl.when(before >= 0)
        def _():
            block(1, which, before, c, before).wait_recv()
            if forward:

                @pl.when(has_right)
                def _():
                    block(1, which, before, c, spot + 1).start()

        @pl.when(after < n_seq)
        def _():
            block(0, which, after, c, after).wait_recv()
            if forward:

                @pl.when(has_left)
                def _():
                    block(0, which, after, c, spot - 1).start()

    if hop:
        for which in range(2):
            for c in range(2):
                take(which, 1, c, True)
        for step in (2, 3):
            for c in range(2):
                take(0, step, c, False)

        def last_values():
            for step in (2, 3):
                for c in range(2):
                    take(1, step, c, False)

    else:

        def chain(i):
            for c in range(2):
                for which in range(2):
                    take(which, i + 1, c, True)

        each(n_seq - 1, chain)

        def last_values():
            pass

    if n_seq <= UNROLL_LIMIT:
        sums, chances = [], []
        for h in range(groups):
            cols = pl.ds(h * span, span)
            keys = kv[0, :, :, cols].reshape(n_seq * rows, span)
            s = lax.dot_general(
                q_ref[:, cols], keys, (((1,), (1,)), ((), ())), preferred_element_type=F32
            ) * (softness_ref[h] / math.sqrt(span))
            top = jnp.max(s, axis=-1, keepdims=True)
            w = jnp.exp(s - top)
            sums.append(jnp.sum(w, axis=-1, keepdims=True))
            chances.append(w.astype(BF16))
        last_values()
        for h in range(groups):
            cols = pl.ds(h * span, span)
            values = kv[1, :, :, cols].reshape(n_seq * rows, span)
            mixed = jnp.dot(chances[h], values, preferred_element_type=F32)
            heads[:, cols] = (mixed / sums[h]).astype(BF16)
    else:
        for h in range(groups):
            cols = pl.ds(h * span, span)
            factor = softness_ref[h] / math.sqrt(span)

            def first(b, top):
                s = lax.dot_general(
                    q_ref[:, cols], kv[0, b, :, cols], (((1,), (1,)), ((), ())),
                    preferred_element_type=F32,
                ) * factor
                scores[b] = s
                return jnp.maximum(top, jnp.max(s, axis=-1, keepdims=True))

            top = lax.fori_loop(0, n_seq, first, jnp.full((rows, 1), -jnp.inf, F32))

            def second(b, state):
                summed, mixed = state
                w = jnp.exp(scores[b] - top)
                mixed = mixed + jnp.dot(
                    w.astype(BF16), kv[1, b, :, cols], preferred_element_type=F32
                )
                return summed + jnp.sum(w, axis=-1, keepdims=True), mixed

            summed, mixed = lax.fori_loop(
                0, n_seq, second, (jnp.zeros((rows, 1), F32), jnp.zeros((rows, span), F32))
            )
            heads[:, cols] = (mixed / summed).astype(BF16)

    loads[3].wait()
    rs_pieces = [pl.ds(i * (rows // RS_PIECES), rows // RS_PIECES) for i in range(RS_PIECES)]

    def share(owner):
        cols = pl.ds(pl.multiple_of(owner * part, part), part)
        return jnp.dot(heads[...], wo[:, cols], preferred_element_type=F32)

    if paired:
        quarter = rows // len(rs_pieces)

        def reduce(lane, piece, target):
            return remote(
                out_send.at[lane, piece], out_recv.at[lane, piece],
                rs_send.at[lane, piece.start // quarter], rs_recv.at[lane, piece.start // quarter],
                "mp", target,
            )

        out_send[0] = share(cross).astype(BF16)
        for piece in rs_pieces:
            send = reduce(0, piece, near)
            send.start()
            sends.append(send)
        for_far = share(far)
        for piece in rs_pieces:
            reduce(0, piece, near).wait_recv()
            low = piece.start
            out_send[2, piece] = (
                for_far[low : low + quarter] + out_recv[0, piece].astype(F32)
            ).astype(BF16)
            send = reduce(2, piece, far)
            send.start()
            sends.append(send)
        out_send[1] = share(near).astype(BF16)
        for piece in rs_pieces:
            send = reduce(1, piece, near)
            send.start()
            sends.append(send)
        own = share(me) + xg[me].astype(F32)
        for piece in rs_pieces:
            reduce(1, piece, near).wait_recv()
        own = own + out_recv[1].astype(F32)
        for piece in rs_pieces:
            reduce(2, piece, far).wait_recv()
            low = piece.start
            out_ref[piece, :] = (
                own[low : low + quarter] + out_recv[2, piece].astype(F32)
            ).astype(BF16)
    else:
        for step in range(1, n_mp):
            peer = lax.rem(me + step, n_mp)
            out_send[step] = share(peer).astype(BF16)
            send = remote(
                out_send.at[step], out_recv.at[step], rs_send.at[step, 0], rs_recv.at[step, 0], "mp", peer
            )
            send.start()
            sends.append(send)
        own = share(me) + xg[me].astype(F32)
        for step in range(1, n_mp):
            remote(
                out_send.at[step], out_recv.at[step], rs_send.at[step, 0], rs_recv.at[step, 0], "mp", me
            ).wait_recv()
            own = own + out_recv[step].astype(F32)
        out_ref[...] = own.astype(BF16)

    for send in sends:
        send.wait_send()

    def drain(b):
        for which in range(2):
            for c in range(2):
                to_right = (b == spot) | (b == spot - 1) if hop else b <= spot
                to_left = (b == spot) | (b == spot + 1) if hop else b >= spot

                @pl.when(has_right & to_right)
                def _():
                    block(1, which, b, c, spot + 1).wait_send()

                @pl.when(has_left & to_left)
                def _():
                    block(0, which, b, c, spot - 1).wait_send()

                if hop:

                    @pl.when(ends & (b == spot))
                    def _():
                        block(2, which, b, c, n_seq - 1 - spot).wait_send()

    each(n_seq, drain)


def per_device(n_mp, n_seq, x, gain, wq, wk, wv, softness, wo):
    rows, part = x.shape
    features, head_cols = wq.shape
    span_rows = n_seq if n_seq > UNROLL_LIMIT else 1
    any_space = pl.BlockSpec(memory_space=pl.ANY)
    vmem = pl.BlockSpec(memory_space=pltpu.VMEM)
    slots = max(n_mp, 3)
    return pl.pallas_call(
        functools.partial(kernel, n_mp, n_seq),
        out_shape=pltpu.VMEM((rows, part), BF16),
        in_specs=[
            any_space, any_space, any_space, any_space, any_space, any_space, any_space,
        ],
        out_specs=vmem,
        scratch_shapes=[
            pltpu.SMEM(softness.shape, F32),
            pltpu.VMEM((1, features), F32),
            pltpu.VMEM((n_mp, rows, part), BF16),
            pltpu.VMEM((features, head_cols), BF16),
            pltpu.VMEM((features, head_cols), BF16),
            pltpu.VMEM((features, head_cols), BF16),
            pltpu.VMEM((head_cols, features), BF16),
            pltpu.VMEM((rows, features), BF16),
            pltpu.VMEM((rows, head_cols), BF16),
            pltpu.VMEM((2, n_seq, rows, head_cols), BF16),
            pltpu.VMEM((span_rows, rows, rows), F32),
            pltpu.VMEM((rows, head_cols), BF16),
            pltpu.VMEM((slots, rows, part), BF16),
            pltpu.VMEM((slots, rows, part), BF16),
            pltpu.SemaphoreType.DMA((2,)),
            pltpu.SemaphoreType.DMA((4,)),
            pltpu.SemaphoreType.DMA,
            pltpu.SemaphoreType.DMA((slots, 2)),
            pltpu.SemaphoreType.DMA((slots, 2)),
            pltpu.SemaphoreType.DMA((3, 2, n_seq, 2)),
            pltpu.SemaphoreType.DMA((2, n_seq, 2)),
            pltpu.SemaphoreType.DMA((slots, RS_PIECES)),
            pltpu.SemaphoreType.DMA((slots, RS_PIECES)),
        ],
        compiler_params=pltpu.CompilerParams(collective_id=0, has_side_effects=True),
    )(softness, x, gain.reshape(1, features), wq, wk, wv, wo)


def line_kernel(
    softness_hbm, x_hbm, gain_hbm, wq_hbm, wk_hbm, wv_hbm, wo_hbm, out_ref,
    softness_ref, gain_ref, xg, xe, wq, wkv, wo, normed, q_ref, kv, heads,
    go_sem, up_sem, small_sem, w_sem, x_sem, xg_send, xg_recv, kv_send, kv_recv,
    wo_send, wo_recv, h_send, h_recv, e_send, e_recv,
):
    n_mp, n_seq = xg.shape[0], kv.shape[1]
    me = lax.axis_index("mp")
    spot = lax.axis_index("seq")
    group = lax.axis_index("groups")
    other = 1 - group
    rows, part = x_hbm.shape
    head_cols = wq_hbm.shape[1]
    groups = softness_hbm.shape[0]
    span = head_cols // groups
    features = n_mp * part
    last = n_seq - 1
    has_left = spot > 0
    has_right = spot < last
    is_first = spot == 0
    is_last = spot == last
    at_end = is_first | is_last
    opposite = last - spot
    odd = lax.rem(me, 2)
    is_odd = odd == 1
    is_even = odd == 0
    near = me + 1 - 2 * odd
    far = lax.rem(me + 2, n_mp)
    cross = lax.rem(near + 2, n_mp)
    even_me = me - odd
    odd_me = even_me + 1

    def columns(owner):
        return pl.ds(pl.multiple_of(owner * part, part), part)

    own_x = pltpu.make_async_copy(x_hbm, xg.at[me], x_sem)
    own_x.start()

    barrier = pltpu.get_barrier_semaphore()

    def greet(**where):
        pl.semaphore_signal(barrier, inc=1, device_id=where, device_id_type=MESH)

    @pl.when(is_odd)
    def _():
        greet(mp=far)

    @pl.when(is_even)
    def _():
        greet(mp=near)
        greet(mp=cross)

    greet(groups=other, mp=odd_me)
    for plane in range(n_seq):

        @pl.when(plane > spot)
        def _():
            greet(seq=plane, mp=odd_me)

        @pl.when(plane < spot)
        def _():
            greet(seq=plane, mp=even_me)

    smalls = [
        pltpu.make_async_copy(gain_hbm, gain_ref, small_sem.at[0]),
        pltpu.make_async_copy(softness_hbm, softness_ref, small_sem.at[1]),
    ]
    for small in smalls:
        small.start()
    loads = [
        pltpu.make_async_copy(src, dst, w_sem.at[i])
        for i, (src, dst) in enumerate(
            (
                (wk_hbm, wkv.at[:, pl.ds(0, head_cols)]),
                (wv_hbm, wkv.at[:, pl.ds(head_cols, head_cols)]),
                (wq_hbm, wq),
                (wo_hbm.at[:, columns(me)], wo.at[me]),
            )
        )
    ]
    for load in loads:
        load.start()

    @pl.when(is_odd)
    def _():
        pl.semaphore_wait(barrier, n_mp - 1 + 2 + 2 * spot)
        pl.semaphore_signal(go_sem, inc=1, device_id={"mp": near}, device_id_type=MESH)

    @pl.when(is_even)
    def _():
        pl.semaphore_wait(go_sem, 1)

    piece_rows = rows // X_PIECES
    half = rows // 2
    halves = [pl.ds(0, half), pl.ds(half, half)]
    pieces = [pl.ds(c * piece_rows, piece_rows) for c in range(X_PIECES)]
    sends = []

    def gather(lane, c, source, target):
        slot = xg.at[source, pieces[c]]
        return remote(slot, slot, xg_send.at[lane, c], xg_recv.at[lane, c], "mp", target)

    for lane, peer in ((0, far), (1, near)):
        for c, piece in enumerate(pieces):
            send = remote(
                x_hbm.at[piece], xg.at[me, piece],
                xg_send.at[lane, c], xg_recv.at[lane, c], "mp", peer,
            )
            send.start()
            sends.append(send)
    own_x.wait()
    for small in smalls:
        small.wait()

    def relay_far(c):
        gather(0, c, far, far).wait_recv()
        relay = gather(2, c, far, near)
        relay.start()
        sends.append(relay)

    def gathered(c):
        gather(1, c, near, near).wait_recv()
        gather(2, c, cross, near).wait_recv()

    def normalize(c, held):
        piece = pieces[c]
        total = jnp.zeros((piece_rows, 1), F32)
        for j in range(n_mp):
            total = total + jnp.sum(held[j, piece, :].astype(F32), axis=-1, keepdims=True)
        average = total / features
        square = jnp.zeros((piece_rows, 1), F32)
        for j in range(n_mp):
            off = held[j, piece, :].astype(F32) - average
            square = square + jnp.sum(off * off, axis=-1, keepdims=True)
        inverse = lax.rsqrt(square / features + 1e-05)
        for j in range(n_mp):
            cols = pl.ds(j * part, part)
            off = held[j, piece, :].astype(F32) - average
            normed[piece, cols] = (off * inverse * gain_ref[:, cols]).astype(BF16)

    def know_later_planes(when):
        @pl.when(when & is_even)
        def _():
            pl.semaphore_wait(barrier, 2 * (last - spot))
            pl.semaphore_signal(up_sem, inc=1, device_id={"mp": near}, device_id_type=MESH)

        @pl.when(when & is_odd)
        def _():
            pl.semaphore_wait(up_sem, 1)

    def end_piece(lane, c, source, target, axis="mp"):
        slot = xe.at[source, pieces[c]]
        return remote(slot, slot, e_send.at[lane, c], e_recv.at[lane, c], axis, target)

    def to_other_end(c):
        return remote(
            x_hbm.at[pieces[c]], xe.at[me, pieces[c]],
            e_send.at[3, c], e_recv.at[3, c], "seq", opposite,
        )

    def send_to_other_end(when):
        @pl.when(when)
        def _():
            for c in range(X_PIECES):
                to_other_end(c).start()

    def block(which, owner, c, target):
        slot = kv.at[which, owner, halves[c]]
        return remote(
            slot, slot, kv_send.at[which, target, c], kv_recv.at[which, owner, c], "seq", target
        )

    def project(c, owner):
        both = jnp.dot(normed[halves[c], :], wkv[...], preferred_element_type=F32).astype(BF16)
        kv[0, owner, halves[c]] = both[:, :head_cols]
        kv[1, owner, halves[c]] = both[:, head_cols:]

    def launch(target, c, when):
        @pl.when(when)
        def _():
            for which in range(2):
                block(which, spot, c, target).start()

    exit_rows = head_cols // 2

    def exit_half(lane, source, rows_of, target, axis):
        there = pl.ds(pl.multiple_of(rows_of * exit_rows, exit_rows), exit_rows)
        slot = wo.at[source, there]
        return remote(slot, slot, wo_send.at[lane], wo_recv.at[lane], axis, target)

    near_exit = remote(
        wo_hbm.at[:, columns(near)], wo.at[me], wo_send.at[0], wo_recv.at[0], "mp", near
    )
    mine = pl.ds(pl.multiple_of(group * exit_rows, exit_rows), exit_rows)
    exits = [
        remote(
            wo_hbm.at[mine, columns(peer)], wo.at[me, mine],
            wo_send.at[lane], wo_recv.at[lane], "mp", peer,
        )
        for lane, peer in ((1, far), (2, cross))
    ] + [near_exit]

    send_to_other_end(is_last)
    for c in range(X_PIECES):
        relay_far(c)
    for send in exits:
        send.start()
        sends.append(send)
    know_later_planes(is_first)
    send_to_other_end(is_first)
    for c in range(X_PIECES):
        gathered(c)
        normalize(c, xg)
        done = (c + 1) * piece_rows
        if done == half:
            loads[0].wait()
            loads[1].wait()
            project(0, spot)
            launch(0, 0, has_left & has_right)
    project(1, spot)
    launch(0, 1, has_left & has_right)
    know_later_planes(has_left & has_right)
    for target in range(1, n_seq):
        for c in range(2):
            launch(target, c, spot != target if target < last else has_left & has_right)

    loads[2].wait()
    q_ref[...] = jnp.dot(normed[...], wq[...], preferred_element_type=F32).astype(BF16)

    def weigh(queries, keys, h):
        s = lax.dot_general(
            queries, keys, (((1,), (1,)), ((), ())), preferred_element_type=F32
        ) * (softness_ref[h] / math.sqrt(span))
        top = jnp.max(s, axis=-1, keepdims=True)
        w = jnp.exp(s - top)
        return jnp.sum(w, axis=-1, keepdims=True), w.astype(BF16)

    head = [pl.ds(h * span, span) for h in range(groups)]
    def exchanged(b):
        ends = (0, last)
        return (spot != b) & (spot != last - b) if b in ends else spot != b

    def take(which):
        for owner in range(n_seq):

            @pl.when(exchanged(owner))
            def _():
                for c in range(2):
                    block(which, owner, c, owner).wait_recv()

    def pass_exit(lane, source):
        exit_half(lane, source, group, source, "mp").wait_recv()
        send = exit_half(lane + 2, source, group, other, "groups")
        send.start()
        sends.append(send)

    @pl.when(at_end)
    def _():
        for c in range(X_PIECES):
            to_other_end(c).wait_recv()
            end_piece(0, c, me, far).start()
            end_piece(1, c, me, near).start()

    pass_exit(1, far)

    @pl.when(at_end)
    def _():
        for c in range(X_PIECES):
            end_piece(0, c, far, far).wait_recv()
            end_piece(2, c, far, near).start()

    pass_exit(2, cross)

    @pl.when(at_end)
    def _():
        for c in range(X_PIECES):
            end_piece(1, c, near, near).wait_recv()
            end_piece(2, c, cross, near).wait_recv()
            normalize(c, xe)
            done = (c + 1) * piece_rows
            if done % half == 0:
                project(done // half - 1, opposite)

    def share(lane, h, source, target):
        slot = heads.at[source, :, head[h]]
        return remote(slot, slot, h_send.at[lane, h], h_recv.at[lane, h], "mp", target)

    even_peer = lax.rem(even_me + 2, n_mp)
    odd_peer = even_peer + 1

    def give(h, mixed):
        heads[me, :, head[h]] = mixed.astype(BF16)
        share(odd, h, me, even_peer).start()

    take(0)
    known = []
    for h in range(groups):
        keys = kv[0, :, :, head[h]].reshape(n_seq * rows, span)
        known.append(weigh(q_ref[:, head[h]], keys, h))
    take(1)
    for h in range(groups):
        values = kv[1, :, :, head[h]].reshape(n_seq * rows, span)
        summed, w = known[h]
        give(h, jnp.dot(w, values, preferred_element_type=F32) / summed)

    for h in range(groups):
        sends.append(share(odd, h, me, even_peer))
        for lane, target in ((1 - odd, odd_peer), (2, near)):
            send = share(lane, h, me, target)
            send.start()
            sends.append(send)

    loads[3].wait()
    total = xg[me].astype(F32) + jnp.dot(heads[me], wo[me], preferred_element_type=F32)
    near_exit.wait_recv()
    for lane, source in ((1, far), (2, cross)):
        exit_half(lane + 2, source, other, other, "groups").wait_recv()
    for lane, source in ((2, near), (0, far), (1, cross)):
        for h in range(groups):
            share(lane, h, source, source).wait_recv()
        total = total + jnp.dot(heads[source], wo[source], preferred_element_type=F32)
    out_ref[...] = total.astype(BF16)

    for send in sends:
        send.wait_send()

    for target in range(n_seq):

        @pl.when(exchanged(target))
        def _():
            for which in range(2):
                for c in range(2):
                    block(which, spot, c, target).wait_send()

    @pl.when(at_end)
    def _():
        for c in range(X_PIECES):
            to_other_end(c).wait_send()
            end_piece(0, c, me, far).wait_send()
            end_piece(1, c, me, near).wait_send()
            end_piece(2, c, far, near).wait_send()


def line_call(n_mp, n_seq, x, gain, wq, wk, wv, softness, wo):
    rows, part = x.shape
    features, head_cols = wq.shape
    heads = softness.shape[0]
    any_space = pl.BlockSpec(memory_space=pl.ANY)
    return pl.pallas_call(
        line_kernel,
        out_shape=pltpu.VMEM((rows, part), BF16),
        in_specs=[any_space] * 7,
        out_specs=pl.BlockSpec(memory_space=pltpu.VMEM),
        scratch_shapes=[
            pltpu.SMEM(softness.shape, F32),
            pltpu.VMEM((1, features), F32),
            pltpu.VMEM((n_mp, rows, part), BF16),
            pltpu.VMEM((n_mp, rows, part), BF16),
            pltpu.VMEM((features, head_cols), BF16),
            pltpu.VMEM((features, 2 * head_cols), BF16),
            pltpu.VMEM((n_mp, head_cols, part), BF16),
            pltpu.VMEM((rows, features), BF16),
            pltpu.VMEM((rows, head_cols), BF16),
            pltpu.VMEM((2, n_seq, rows, head_cols), BF16),
            pltpu.VMEM((n_mp, rows, head_cols), BF16),
            pltpu.SemaphoreType.REGULAR,
            pltpu.SemaphoreType.REGULAR,
            pltpu.SemaphoreType.DMA((2,)),
            pltpu.SemaphoreType.DMA((4,)),
            pltpu.SemaphoreType.DMA,
            pltpu.SemaphoreType.DMA((3, X_PIECES)),
            pltpu.SemaphoreType.DMA((3, X_PIECES)),
            pltpu.SemaphoreType.DMA((2, n_seq, 2)),
            pltpu.SemaphoreType.DMA((2, n_seq, 2)),
            pltpu.SemaphoreType.DMA((5,)),
            pltpu.SemaphoreType.DMA((5,)),
            pltpu.SemaphoreType.DMA((3, heads)),
            pltpu.SemaphoreType.DMA((3, heads)),
            pltpu.SemaphoreType.DMA((4, X_PIECES)),
            pltpu.SemaphoreType.DMA((4, X_PIECES)),
        ],
        compiler_params=pltpu.CompilerParams(
            collective_id=0, has_side_effects=True, vmem_limit_bytes=VMEM_BYTES
        ),
    )(softness, x, gain.reshape(1, features), wq, wk, wv, wo)


def solution(mesh):
    short = mesh.shape["mp"] == 4 and mesh.shape["seq"] == 4 and mesh.shape["groups"] == 2
    return jax.shard_map(
        functools.partial(line_call if short else per_device, mesh.shape["mp"], mesh.shape["seq"]),
        mesh=mesh,
        in_specs=(
            P(("groups", "seq"), "mp"),
            P(),
            P(None, "mp"),
            P(None, "mp"),
            P(None, "mp"),
            P("mp"),
            P("mp", None),
        ),
        out_specs=P(("groups", "seq"), "mp"),
        check_vma=False,
    )
```

```python
import functools
import math

import jax
import jax.numpy as jnp
from jax import lax
from jax.experimental import pallas as pl
from jax.experimental.pallas import tpu as pltpu
from jax.sharding import PartitionSpec as P

MESH = pl.DeviceIdType.MESH
F32 = jnp.float32
BF16 = jnp.bfloat16
UNROLL_LIMIT = 8
RS_PIECES = 2
X_PIECES = 4
VMEM_BYTES = 60 * 1024 * 1024


def remote(src, dst, send_sem, recv_sem, axis, index):
    return pltpu.make_async_remote_copy(
        src_ref=src,
        dst_ref=dst,
        send_sem=send_sem,
        recv_sem=recv_sem,
        device_id={axis: index},
        device_id_type=MESH,
    )


def each(count, body):
    if count <= UNROLL_LIMIT:
        for i in range(count):
            body(i)
    else:
        lax.fori_loop(0, count, lambda i, c: (body(i), c)[1], 0)


def kernel(
    n_mp,
    n_seq,
    softness_hbm,
    x_hbm,
    gain_hbm,
    wq_hbm,
    wk_hbm,
    wv_hbm,
    wo_hbm,
    out_ref,
    softness_ref,
    gain_ref,
    xg,
    wq,
    wk,
    wv,
    wo,
    normed,
    q_ref,
    kv,
    scores,
    heads,
    out_send,
    out_recv,
    small_sem,
    w_sem,
    x_sem,
    xg_send,
    xg_recv,
    kv_send,
    kv_recv,
    rs_send,
    rs_recv,
):
    me = lax.axis_index("mp")
    spot = lax.axis_index("seq")
    rows, part = x_hbm.shape
    head_cols = wq_hbm.shape[1]
    groups = softness_hbm.shape[0]
    span = head_cols // groups
    paired = n_mp == 4
    has_left = spot > 0
    has_right = spot < n_seq - 1
    hop = n_seq == 4
    ends = (spot == 0) | (spot == n_seq - 1)

    own_x = pltpu.make_async_copy(x_hbm, xg.at[me], x_sem)
    own_x.start()
    smalls = [
        pltpu.make_async_copy(gain_hbm, gain_ref, small_sem.at[0]),
        pltpu.make_async_copy(softness_hbm, softness_ref, small_sem.at[1]),
    ]
    for small in smalls:
        small.start()
    loads = [
        pltpu.make_async_copy(src, dst, w_sem.at[i])
        for i, (src, dst) in enumerate(((wk_hbm, wk), (wv_hbm, wv), (wq_hbm, wq), (wo_hbm, wo)))
    ]
    for load in loads:
        load.start()

    barrier = pltpu.get_barrier_semaphore()
    for step in range(1, n_mp):
        pl.semaphore_signal(
            barrier, inc=1, device_id={"mp": lax.rem(me + step, n_mp)}, device_id_type=MESH
        )

    @pl.when(has_left)
    def _():
        pl.semaphore_signal(barrier, inc=1, device_id={"seq": spot - 1}, device_id_type=MESH)

    @pl.when(has_right)
    def _():
        pl.semaphore_signal(barrier, inc=1, device_id={"seq": spot + 1}, device_id_type=MESH)

    greeted = n_mp - 1 + has_left.astype(jnp.int32) + has_right.astype(jnp.int32)
    if hop:

        @pl.when(ends)
        def _():
            pl.semaphore_signal(
                barrier, inc=1, device_id={"seq": n_seq - 1 - spot}, device_id_type=MESH
            )

        greeted = greeted + ends.astype(jnp.int32)
    pl.semaphore_wait(barrier, greeted)

    half = rows // 2
    pieces = [pl.ds(0, half), pl.ds(half, half)]
    near = me + 1 - 2 * lax.rem(me, 2)
    far = lax.rem(me + 2, n_mp)
    cross = lax.rem(near + 2, n_mp)
    sends = []

    def gather(lane, c, source, target):
        slot = xg.at[source, pieces[c]]
        return remote(slot, slot, xg_send.at[lane, c], xg_recv.at[lane, c], "mp", target)

    if paired:
        for lane, peer in ((0, far), (1, near)):
            for c, piece in enumerate(pieces):
                send = remote(
                    x_hbm.at[piece], xg.at[me, piece],
                    xg_send.at[lane, c], xg_recv.at[lane, c], "mp", peer,
                )
                send.start()
                sends.append(send)
    else:
        for c, piece in enumerate(pieces):
            for step in range(1, n_mp):
                send = remote(
                    x_hbm.at[piece], xg.at[me, piece],
                    xg_send.at[step, c], xg_recv.at[step, c], "mp", lax.rem(me + step, n_mp),
                )
                send.start()
                sends.append(send)
    own_x.wait()
    for small in smalls:
        small.wait()

    def relay_far(c):
        if paired:
            gather(0, c, far, far).wait_recv()
            relay = gather(2, c, far, near)
            relay.start()
            sends.append(relay)

    def gathered(c):
        if paired:
            gather(1, c, near, near).wait_recv()
            gather(2, c, cross, near).wait_recv()
        else:
            for step in range(1, n_mp):
                source = lax.rem(me - step + n_mp, n_mp)
                gather(step, c, source, source).wait_recv()

    features = n_mp * part

    def normalize(c):
        piece = pieces[c]
        total = jnp.zeros((half, 1), F32)
        for j in range(n_mp):
            total = total + jnp.sum(xg[j, piece, :].astype(F32), axis=-1, keepdims=True)
        average = total / features
        square = jnp.zeros((half, 1), F32)
        for j in range(n_mp):
            off = xg[j, piece, :].astype(F32) - average
            square = square + jnp.sum(off * off, axis=-1, keepdims=True)
        inverse = lax.rsqrt(square / features + 1e-05)
        for j in range(n_mp):
            cols = pl.ds(j * part, part)
            off = xg[j, piece, :].astype(F32) - average
            normed[piece, cols] = (off * inverse * gain_ref[:, cols]).astype(BF16)

    def block(way, which, owner, c, target):
        slot = kv.at[which, owner, pieces[c]]
        return remote(
            slot, slot, kv_send.at[way, which, owner, c], kv_recv.at[which, owner, c], "seq", target
        )

    def project(which, weight, c):
        kv[which, spot, pieces[c]] = jnp.dot(
            normed[pieces[c], :], weight[...], preferred_element_type=F32
        ).astype(BF16)
        launch(which, c)

    def launch(which, c):
        @pl.when(has_right)
        def _():
            block(1, which, spot, c, spot + 1).start()

        @pl.when(has_left)
        def _():
            block(0, which, spot, c, spot - 1).start()

        if hop:

            @pl.when(ends)
            def _():
                block(2, which, spot, c, n_seq - 1 - spot).start()

    relay_far(0)
    gathered(0)
    normalize(0)
    relay_far(1)
    loads[0].wait()
    project(0, wk, 0)
    gathered(1)
    normalize(1)
    project(0, wk, 1)
    loads[1].wait()
    kv[1, spot] = jnp.dot(normed[...], wv[...], preferred_element_type=F32).astype(BF16)
    for c in range(2):
        launch(1, c)
    loads[2].wait()
    q_ref[...] = jnp.dot(normed[...], wq[...], preferred_element_type=F32).astype(BF16)

    def take(which, step, c, forward):
        before = spot - step
        after = spot + step

        @pl.when(before >= 0)
        def _():
            block(1, which, before, c, before).wait_recv()
            if forward:

                @pl.when(has_right)
                def _():
                    block(1, which, before, c, spot + 1).start()

        @pl.when(after < n_seq)
        def _():
            block(0, which, after, c, after).wait_recv()
            if forward:

                @pl.when(has_left)
                def _():
                    block(0, which, after, c, spot - 1).start()

    if hop:
        for which in range(2):
            for c in range(2):
                take(which, 1, c, True)
        for step in (2, 3):
            for c in range(2):
                take(0, step, c, False)

        def last_values():
            for step in (2, 3):
                for c in range(2):
                    take(1, step, c, False)

    else:

        def chain(i):
            for c in range(2):
                for which in range(2):
                    take(which, i + 1, c, True)

        each(n_seq - 1, chain)

        def last_values():
            pass

    if n_seq <= UNROLL_LIMIT:
        sums, chances = [], []
        for h in range(groups):
            cols = pl.ds(h * span, span)
            keys = kv[0, :, :, cols].reshape(n_seq * rows, span)
            s = lax.dot_general(
                q_ref[:, cols], keys, (((1,), (1,)), ((), ())), preferred_element_type=F32
            ) * (softness_ref[h] / math.sqrt(span))
            top = jnp.max(s, axis=-1, keepdims=True)
            w = jnp.exp(s - top)
            sums.append(jnp.sum(w, axis=-1, keepdims=True))
            chances.append(w.astype(BF16))
        last_values()
        for h in range(groups):
            cols = pl.ds(h * span, span)
            values = kv[1, :, :, cols].reshape(n_seq * rows, span)
            mixed = jnp.dot(chances[h], values, preferred_element_type=F32)
            heads[:, cols] = (mixed / sums[h]).astype(BF16)
    else:
        for h in range(groups):
            cols = pl.ds(h * span, span)
            factor = softness_ref[h] / math.sqrt(span)

            def first(b, top):
                s = lax.dot_general(
                    q_ref[:, cols], kv[0, b, :, cols], (((1,), (1,)), ((), ())),
                    preferred_element_type=F32,
                ) * factor
                scores[b] = s
                return jnp.maximum(top, jnp.max(s, axis=-1, keepdims=True))

            top = lax.fori_loop(0, n_seq, first, jnp.full((rows, 1), -jnp.inf, F32))

            def second(b, state):
                summed, mixed = state
                w = jnp.exp(scores[b] - top)
                mixed = mixed + jnp.dot(
                    w.astype(BF16), kv[1, b, :, cols], preferred_element_type=F32
                )
                return summed + jnp.sum(w, axis=-1, keepdims=True), mixed

            summed, mixed = lax.fori_loop(
                0, n_seq, second, (jnp.zeros((rows, 1), F32), jnp.zeros((rows, span), F32))
            )
            heads[:, cols] = (mixed / summed).astype(BF16)

    loads[3].wait()
    rs_pieces = [pl.ds(i * (rows // RS_PIECES), rows // RS_PIECES) for i in range(RS_PIECES)]

    def share(owner):
        cols = pl.ds(pl.multiple_of(owner * part, part), part)
        return jnp.dot(heads[...], wo[:, cols], preferred_element_type=F32)

    if paired:
        quarter = rows // len(rs_pieces)

        def reduce(lane, piece, target):
            return remote(
                out_send.at[lane, piece], out_recv.at[lane, piece],
                rs_send.at[lane, piece.start // quarter], rs_recv.at[lane, piece.start // quarter],
                "mp", target,
            )

        out_send[0] = share(cross).astype(BF16)
        for piece in rs_pieces:
            send = reduce(0, piece, near)
            send.start()
            sends.append(send)
        for_far = share(far)
        for piece in rs_pieces:
            reduce(0, piece, near).wait_recv()
            low = piece.start
            out_send[2, piece] = (
                for_far[low : low + quarter] + out_recv[0, piece].astype(F32)
            ).astype(BF16)
            send = reduce(2, piece, far)
            send.start()
            sends.append(send)
        out_send[1] = share(near).astype(BF16)
        for piece in rs_pieces:
            send = reduce(1, piece, near)
            send.start()
            sends.append(send)
        own = share(me) + xg[me].astype(F32)
        for piece in rs_pieces:
            reduce(1, piece, near).wait_recv()
        own = own + out_recv[1].astype(F32)
        for piece in rs_pieces:
            reduce(2, piece, far).wait_recv()
            low = piece.start
            out_ref[piece, :] = (
                own[low : low + quarter] + out_recv[2, piece].astype(F32)
            ).astype(BF16)
    else:
        for step in range(1, n_mp):
            peer = lax.rem(me + step, n_mp)
            out_send[step] = share(peer).astype(BF16)
            send = remote(
                out_send.at[step], out_recv.at[step], rs_send.at[step, 0], rs_recv.at[step, 0], "mp", peer
            )
            send.start()
            sends.append(send)
        own = share(me) + xg[me].astype(F32)
        for step in range(1, n_mp):
            remote(
                out_send.at[step], out_recv.at[step], rs_send.at[step, 0], rs_recv.at[step, 0], "mp", me
            ).wait_recv()
            own = own + out_recv[step].astype(F32)
        out_ref[...] = own.astype(BF16)

    for send in sends:
        send.wait_send()

    def drain(b):
        for which in range(2):
            for c in range(2):
                to_right = (b == spot) | (b == spot - 1) if hop else b <= spot
                to_left = (b == spot) | (b == spot + 1) if hop else b >= spot

                @pl.when(has_right & to_right)
                def _():
                    block(1, which, b, c, spot + 1).wait_send()

                @pl.when(has_left & to_left)
                def _():
                    block(0, which, b, c, spot - 1).wait_send()

                if hop:

                    @pl.when(ends & (b == spot))
                    def _():
                        block(2, which, b, c, n_seq - 1 - spot).wait_send()

    each(n_seq, drain)


def per_device(n_mp, n_seq, x, gain, wq, wk, wv, softness, wo):
    rows, part = x.shape
    features, head_cols = wq.shape
    span_rows = n_seq if n_seq > UNROLL_LIMIT else 1
    any_space = pl.BlockSpec(memory_space=pl.ANY)
    vmem = pl.BlockSpec(memory_space=pltpu.VMEM)
    slots = max(n_mp, 3)
    return pl.pallas_call(
        functools.partial(kernel, n_mp, n_seq),
        out_shape=pltpu.VMEM((rows, part), BF16),
        in_specs=[
            any_space, any_space, any_space, any_space, any_space, any_space, any_space,
        ],
        out_specs=vmem,
        scratch_shapes=[
            pltpu.SMEM(softness.shape, F32),
            pltpu.VMEM((1, features), F32),
            pltpu.VMEM((n_mp, rows, part), BF16),
            pltpu.VMEM((features, head_cols), BF16),
            pltpu.VMEM((features, head_cols), BF16),
            pltpu.VMEM((features, head_cols), BF16),
            pltpu.VMEM((head_cols, features), BF16),
            pltpu.VMEM((rows, features), BF16),
            pltpu.VMEM((rows, head_cols), BF16),
            pltpu.VMEM((2, n_seq, rows, head_cols), BF16),
            pltpu.VMEM((span_rows, rows, rows), F32),
            pltpu.VMEM((rows, head_cols), BF16),
            pltpu.VMEM((slots, rows, part), BF16),
            pltpu.VMEM((slots, rows, part), BF16),
            pltpu.SemaphoreType.DMA((2,)),
            pltpu.SemaphoreType.DMA((4,)),
            pltpu.SemaphoreType.DMA,
            pltpu.SemaphoreType.DMA((slots, 2)),
            pltpu.SemaphoreType.DMA((slots, 2)),
            pltpu.SemaphoreType.DMA((3, 2, n_seq, 2)),
            pltpu.SemaphoreType.DMA((2, n_seq, 2)),
            pltpu.SemaphoreType.DMA((slots, RS_PIECES)),
            pltpu.SemaphoreType.DMA((slots, RS_PIECES)),
        ],
        compiler_params=pltpu.CompilerParams(collective_id=0, has_side_effects=True),
    )(softness, x, gain.reshape(1, features), wq, wk, wv, wo)


def line_kernel(
    softness_hbm, x_hbm, gain_hbm, wq_hbm, wk_hbm, wv_hbm, wo_hbm, out_ref,
    softness_ref, gain_ref, xg, xe, wq, wkv, wo, normed, q_ref, kv, heads,
    go_sem, up_sem, small_sem, w_sem, x_sem, xg_send, xg_recv, kv_send, kv_recv,
    wo_send, wo_recv, h_send, h_recv, e_send, e_recv,
):
    n_mp, n_seq = xg.shape[0], kv.shape[1]
    me = lax.axis_index("mp")
    spot = lax.axis_index("seq")
    group = lax.axis_index("groups")
    other = 1 - group
    rows, part = x_hbm.shape
    head_cols = wq_hbm.shape[1]
    groups = softness_hbm.shape[0]
    span = head_cols // groups
    features = n_mp * part
    last = n_seq - 1
    has_left = spot > 0
    has_right = spot < last
    is_first = spot == 0
    is_last = spot == last
    at_end = is_first | is_last
    opposite = last - spot
    odd = lax.rem(me, 2)
    is_odd = odd == 1
    is_even = odd == 0
    near = me + 1 - 2 * odd
    far = lax.rem(me + 2, n_mp)
    cross = lax.rem(near + 2, n_mp)
    even_me = me - odd
    odd_me = even_me + 1

    def columns(owner):
        return pl.ds(pl.multiple_of(owner * part, part), part)

    own_x = pltpu.make_async_copy(x_hbm, xg.at[me], x_sem)
    own_x.start()

    barrier = pltpu.get_barrier_semaphore()

    def greet(**where):
        pl.semaphore_signal(barrier, inc=1, device_id=where, device_id_type=MESH)

    @pl.when(is_odd)
    def _():
        greet(mp=far)

    @pl.when(is_even)
    def _():
        greet(mp=near)
        greet(mp=cross)

    greet(groups=other, mp=odd_me)
    for plane in range(n_seq):

        @pl.when(plane > spot)
        def _():
            greet(seq=plane, mp=odd_me)

        @pl.when(plane < spot)
        def _():
            greet(seq=plane, mp=even_me)

    smalls = [
        pltpu.make_async_copy(gain_hbm, gain_ref, small_sem.at[0]),
        pltpu.make_async_copy(softness_hbm, softness_ref, small_sem.at[1]),
    ]
    for small in smalls:
        small.start()
    loads = [
        pltpu.make_async_copy(src, dst, w_sem.at[i])
        for i, (src, dst) in enumerate(
            (
                (wk_hbm, wkv.at[:, pl.ds(0, head_cols)]),
                (wv_hbm, wkv.at[:, pl.ds(head_cols, head_cols)]),
                (wq_hbm, wq),
                (wo_hbm.at[:, columns(me)], wo.at[me]),
            )
        )
    ]
    for load in loads:
        load.start()

    @pl.when(is_odd)
    def _():
        pl.semaphore_wait(barrier, n_mp - 1 + 2 + 2 * spot)
        pl.semaphore_signal(go_sem, inc=1, device_id={"mp": near}, device_id_type=MESH)

    @pl.when(is_even)
    def _():
        pl.semaphore_wait(go_sem, 1)

    piece_rows = rows // X_PIECES
    half = rows // 2
    halves = [pl.ds(0, half), pl.ds(half, half)]
    pieces = [pl.ds(c * piece_rows, piece_rows) for c in range(X_PIECES)]
    sends = []

    def gather(lane, c, source, target):
        slot = xg.at[source, pieces[c]]
        return remote(slot, slot, xg_send.at[lane, c], xg_recv.at[lane, c], "mp", target)

    for lane, peer in ((0, far), (1, near)):
        for c, piece in enumerate(pieces):
            send = remote(
                x_hbm.at[piece], xg.at[me, piece],
                xg_send.at[lane, c], xg_recv.at[lane, c], "mp", peer,
            )
            send.start()
            sends.append(send)
    own_x.wait()
    for small in smalls:
        small.wait()

    def relay_far(c):
        gather(0, c, far, far).wait_recv()
        relay = gather(2, c, far, near)
        relay.start()
        sends.append(relay)

    def gathered(c):
        gather(1, c, near, near).wait_recv()
        gather(2, c, cross, near).wait_recv()

    def normalize(c, held):
        piece = pieces[c]
        total = jnp.zeros((piece_rows, 1), F32)
        for j in range(n_mp):
            total = total + jnp.sum(held[j, piece, :].astype(F32), axis=-1, keepdims=True)
        average = total / features
        square = jnp.zeros((piece_rows, 1), F32)
        for j in range(n_mp):
            off = held[j, piece, :].astype(F32) - average
            square = square + jnp.sum(off * off, axis=-1, keepdims=True)
        inverse = lax.rsqrt(square / features + 1e-05)
        for j in range(n_mp):
            cols = pl.ds(j * part, part)
            off = held[j, piece, :].astype(F32) - average
            normed[piece, cols] = (off * inverse * gain_ref[:, cols]).astype(BF16)

    def know_later_planes(when):
        @pl.when(when & is_even)
        def _():
            pl.semaphore_wait(barrier, 2 * (last - spot))
            pl.semaphore_signal(up_sem, inc=1, device_id={"mp": near}, device_id_type=MESH)

        @pl.when(when & is_odd)
        def _():
            pl.semaphore_wait(up_sem, 1)

    def end_piece(lane, c, source, target, axis="mp"):
        slot = xe.at[source, pieces[c]]
        return remote(slot, slot, e_send.at[lane, c], e_recv.at[lane, c], axis, target)

    def to_other_end(c):
        return remote(
            x_hbm.at[pieces[c]], xe.at[me, pieces[c]],
            e_send.at[3, c], e_recv.at[3, c], "seq", opposite,
        )

    def send_to_other_end(when):
        @pl.when(when)
        def _():
            for c in range(X_PIECES):
                to_other_end(c).start()

    def block(which, owner, c, target, lane=None):
        slot = kv.at[which, owner, halves[c]]
        lane = target if lane is None else lane
        return remote(
            slot, slot, kv_send.at[which, lane, c], kv_recv.at[which, owner, c], "seq", target
        )

    def project(c, owner):
        both = jnp.dot(normed[halves[c], :], wkv[...], preferred_element_type=F32).astype(BF16)
        kv[0, owner, halves[c]] = both[:, :head_cols]
        kv[1, owner, halves[c]] = both[:, head_cols:]

    def launch(target, c, when):
        @pl.when(when)
        def _():
            for which in range(2):
                block(which, spot, c, target).start()

    exit_rows = head_cols // 2

    def exit_half(lane, source, rows_of, target, axis):
        there = pl.ds(pl.multiple_of(rows_of * exit_rows, exit_rows), exit_rows)
        slot = wo.at[source, there]
        return remote(slot, slot, wo_send.at[lane], wo_recv.at[lane], axis, target)

    near_exit = remote(
        wo_hbm.at[:, columns(near)], wo.at[me], wo_send.at[0], wo_recv.at[0], "mp", near
    )
    mine = pl.ds(pl.multiple_of(group * exit_rows, exit_rows), exit_rows)
    exits = [
        remote(
            wo_hbm.at[mine, columns(peer)], wo.at[me, mine],
            wo_send.at[lane], wo_recv.at[lane], "mp", peer,
        )
        for lane, peer in ((1, far), (2, cross))
    ] + [near_exit]

    send_to_other_end(is_last)
    for send in exits:
        send.start()
        sends.append(send)
    for c in range(X_PIECES):
        relay_far(c)
    know_later_planes(is_first)
    send_to_other_end(is_first)
    for c in range(X_PIECES):
        gathered(c)
        normalize(c, xg)
        done = (c + 1) * piece_rows
        if done == half:
            loads[0].wait()
            loads[1].wait()
            project(0, spot)
            launch(0, 0, has_left & has_right)
    project(1, spot)
    launch(0, 1, has_left & has_right)
    know_later_planes(has_left & has_right)
    for c in range(2):
        launch(last, c, spot == last - 1)
    for target in range(1, last):
        for c in range(2):
            launch(target, c, spot < target)
    for target in range(1, last):
        for c in range(2):
            launch(target, c, spot > target)

    loads[2].wait()
    q_ref[...] = jnp.dot(normed[...], wq[...], preferred_element_type=F32).astype(BF16)

    def weigh(queries, keys, h):
        s = lax.dot_general(
            queries, keys, (((1,), (1,)), ((), ())), preferred_element_type=F32
        ) * (softness_ref[h] / math.sqrt(span))
        top = jnp.max(s, axis=-1, keepdims=True)
        w = jnp.exp(s - top)
        return jnp.sum(w, axis=-1, keepdims=True), w.astype(BF16)

    head = [pl.ds(h * span, span) for h in range(groups)]
    passes = spot == last - 1

    @pl.when(passes)
    def _():
        for c in range(2):
            for which in range(2):
                block(which, last - 2, c, last - 2).wait_recv()
                block(which, last - 2, c, last, last - 1).start()

    def exchanged(b):
        ends = (0, last)
        return (spot != b) & (spot != last - b) if b in ends else spot != b

    def take(which):
        for owner in range(n_seq):
            seen = passes if owner == last - 2 else False

            @pl.when(exchanged(owner) & jnp.logical_not(seen))
            def _():
                for c in range(2):
                    block(which, owner, c, owner).wait_recv()

    def pass_exit(lane, source):
        exit_half(lane, source, group, source, "mp").wait_recv()
        send = exit_half(lane + 2, source, group, other, "groups")
        send.start()
        sends.append(send)

    @pl.when(at_end)
    def _():
        for c in range(X_PIECES):
            to_other_end(c).wait_recv()
            end_piece(0, c, me, far).start()
            end_piece(1, c, me, near).start()

    pass_exit(1, far)

    @pl.when(at_end)
    def _():
        for c in range(X_PIECES):
            end_piece(0, c, far, far).wait_recv()
            end_piece(2, c, far, near).start()

    pass_exit(2, cross)

    @pl.when(at_end)
    def _():
        for c in range(X_PIECES):
            end_piece(1, c, near, near).wait_recv()
            end_piece(2, c, cross, near).wait_recv()
            normalize(c, xe)
            done = (c + 1) * piece_rows
            if done % half == 0:
                project(done // half - 1, opposite)

    def share(lane, h, source, target):
        slot = heads.at[source, :, head[h]]
        return remote(slot, slot, h_send.at[lane, h], h_recv.at[lane, h], "mp", target)

    even_peer = lax.rem(even_me + 2, n_mp)
    odd_peer = even_peer + 1

    def give(h, mixed):
        heads[me, :, head[h]] = mixed.astype(BF16)
        share(odd, h, me, even_peer).start()

    take(0)
    known = []
    for h in range(groups):
        keys = kv[0, :, :, head[h]].reshape(n_seq * rows, span)
        known.append(weigh(q_ref[:, head[h]], keys, h))
    take(1)
    for h in range(groups):
        values = kv[1, :, :, head[h]].reshape(n_seq * rows, span)
        summed, w = known[h]
        give(h, jnp.dot(w, values, preferred_element_type=F32) / summed)

    for h in range(groups):
        sends.append(share(odd, h, me, even_peer))
        for lane, target in ((1 - odd, odd_peer), (2, near)):
            send = share(lane, h, me, target)
            send.start()
            sends.append(send)

    loads[3].wait()
    total = xg[me].astype(F32) + jnp.dot(heads[me], wo[me], preferred_element_type=F32)
    near_exit.wait_recv()
    for lane, source in ((1, far), (2, cross)):
        exit_half(lane + 2, source, other, other, "groups").wait_recv()
    for lane, source in ((2, near), (0, far), (1, cross)):
        for h in range(groups):
            share(lane, h, source, source).wait_recv()
        total = total + jnp.dot(heads[source], wo[source], preferred_element_type=F32)
    out_ref[...] = total.astype(BF16)

    for send in sends:
        send.wait_send()

    for target in range(n_seq):

        by_relay = spot == last - 2 if target == last else False

        @pl.when(exchanged(target) & jnp.logical_not(by_relay))
        def _():
            for which in range(2):
                for c in range(2):
                    block(which, spot, c, target).wait_send()

    @pl.when(passes)
    def _():
        for c in range(2):
            for which in range(2):
                block(which, last - 2, c, last, last - 1).wait_send()

    @pl.when(at_end)
    def _():
        for c in range(X_PIECES):
            to_other_end(c).wait_send()
            end_piece(0, c, me, far).wait_send()
            end_piece(1, c, me, near).wait_send()
            end_piece(2, c, far, near).wait_send()


def line_call(n_mp, n_seq, x, gain, wq, wk, wv, softness, wo):
    rows, part = x.shape
    features, head_cols = wq.shape
    heads = softness.shape[0]
    any_space = pl.BlockSpec(memory_space=pl.ANY)
    return pl.pallas_call(
        line_kernel,
        out_shape=pltpu.VMEM((rows, part), BF16),
        in_specs=[any_space] * 7,
        out_specs=pl.BlockSpec(memory_space=pltpu.VMEM),
        scratch_shapes=[
            pltpu.SMEM(softness.shape, F32),
            pltpu.VMEM((1, features), F32),
            pltpu.VMEM((n_mp, rows, part), BF16),
            pltpu.VMEM((n_mp, rows, part), BF16),
            pltpu.VMEM((features, head_cols), BF16),
            pltpu.VMEM((features, 2 * head_cols), BF16),
            pltpu.VMEM((n_mp, head_cols, part), BF16),
            pltpu.VMEM((rows, features), BF16),
            pltpu.VMEM((rows, head_cols), BF16),
            pltpu.VMEM((2, n_seq, rows, head_cols), BF16),
            pltpu.VMEM((n_mp, rows, head_cols), BF16),
            pltpu.SemaphoreType.REGULAR,
            pltpu.SemaphoreType.REGULAR,
            pltpu.SemaphoreType.DMA((2,)),
            pltpu.SemaphoreType.DMA((4,)),
            pltpu.SemaphoreType.DMA,
            pltpu.SemaphoreType.DMA((3, X_PIECES)),
            pltpu.SemaphoreType.DMA((3, X_PIECES)),
            pltpu.SemaphoreType.DMA((2, n_seq, 2)),
            pltpu.SemaphoreType.DMA((2, n_seq, 2)),
            pltpu.SemaphoreType.DMA((5,)),
            pltpu.SemaphoreType.DMA((5,)),
            pltpu.SemaphoreType.DMA((3, heads)),
            pltpu.SemaphoreType.DMA((3, heads)),
            pltpu.SemaphoreType.DMA((4, X_PIECES)),
            pltpu.SemaphoreType.DMA((4, X_PIECES)),
        ],
        compiler_params=pltpu.CompilerParams(
            collective_id=0, has_side_effects=True, vmem_limit_bytes=VMEM_BYTES
        ),
    )(softness, x, gain.reshape(1, features), wq, wk, wv, wo)


def solution(mesh):
    short = mesh.shape["mp"] == 4 and mesh.shape["seq"] == 4 and mesh.shape["groups"] == 2
    return jax.shard_map(
        functools.partial(line_call if short else per_device, mesh.shape["mp"], mesh.shape["seq"]),
        mesh=mesh,
        in_specs=(
            P(("groups", "seq"), "mp"),
            P(),
            P(None, "mp"),
            P(None, "mp"),
            P(None, "mp"),
            P("mp"),
            P("mp", None),
        ),
        out_specs=P(("groups", "seq"), "mp"),
        check_vma=False,
    )
```

```python
import functools
import math

import jax
import jax.numpy as jnp
from jax import lax
from jax.experimental import pallas as pl
from jax.experimental.pallas import tpu as pltpu
from jax.sharding import PartitionSpec as P

MESH = pl.DeviceIdType.MESH
F32 = jnp.float32
BF16 = jnp.bfloat16
UNROLL_LIMIT = 8
RS_PIECES = 2
X_PIECES = 2
VMEM_BYTES = 60 * 1024 * 1024


def remote(src, dst, send_sem, recv_sem, axis, index):
    return pltpu.make_async_remote_copy(
        src_ref=src,
        dst_ref=dst,
        send_sem=send_sem,
        recv_sem=recv_sem,
        device_id={axis: index},
        device_id_type=MESH,
    )


def each(count, body):
    if count <= UNROLL_LIMIT:
        for i in range(count):
            body(i)
    else:
        lax.fori_loop(0, count, lambda i, c: (body(i), c)[1], 0)


def kernel(
    n_mp,
    n_seq,
    softness_hbm,
    x_hbm,
    gain_hbm,
    wq_hbm,
    wk_hbm,
    wv_hbm,
    wo_hbm,
    out_ref,
    softness_ref,
    gain_ref,
    xg,
    wq,
    wk,
    wv,
    wo,
    normed,
    q_ref,
    kv,
    scores,
    heads,
    out_send,
    out_recv,
    small_sem,
    w_sem,
    x_sem,
    xg_send,
    xg_recv,
    kv_send,
    kv_recv,
    rs_send,
    rs_recv,
):
    me = lax.axis_index("mp")
    spot = lax.axis_index("seq")
    rows, part = x_hbm.shape
    head_cols = wq_hbm.shape[1]
    groups = softness_hbm.shape[0]
    span = head_cols // groups
    paired = n_mp == 4
    has_left = spot > 0
    has_right = spot < n_seq - 1
    hop = n_seq == 4
    ends = (spot == 0) | (spot == n_seq - 1)

    own_x = pltpu.make_async_copy(x_hbm, xg.at[me], x_sem)
    own_x.start()
    smalls = [
        pltpu.make_async_copy(gain_hbm, gain_ref, small_sem.at[0]),
        pltpu.make_async_copy(softness_hbm, softness_ref, small_sem.at[1]),
    ]
    for small in smalls:
        small.start()
    loads = [
        pltpu.make_async_copy(src, dst, w_sem.at[i])
        for i, (src, dst) in enumerate(((wk_hbm, wk), (wv_hbm, wv), (wq_hbm, wq), (wo_hbm, wo)))
    ]
    for load in loads:
        load.start()

    barrier = pltpu.get_barrier_semaphore()
    for step in range(1, n_mp):
        pl.semaphore_signal(
            barrier, inc=1, device_id={"mp": lax.rem(me + step, n_mp)}, device_id_type=MESH
        )

    @pl.when(has_left)
    def _():
        pl.semaphore_signal(barrier, inc=1, device_id={"seq": spot - 1}, device_id_type=MESH)

    @pl.when(has_right)
    def _():
        pl.semaphore_signal(barrier, inc=1, device_id={"seq": spot + 1}, device_id_type=MESH)

    greeted = n_mp - 1 + has_left.astype(jnp.int32) + has_right.astype(jnp.int32)
    if hop:

        @pl.when(ends)
        def _():
            pl.semaphore_signal(
                barrier, inc=1, device_id={"seq": n_seq - 1 - spot}, device_id_type=MESH
            )

        greeted = greeted + ends.astype(jnp.int32)
    pl.semaphore_wait(barrier, greeted)

    half = rows // 2
    pieces = [pl.ds(0, half), pl.ds(half, half)]
    near = me + 1 - 2 * lax.rem(me, 2)
    far = lax.rem(me + 2, n_mp)
    cross = lax.rem(near + 2, n_mp)
    sends = []

    def gather(lane, c, source, target):
        slot = xg.at[source, pieces[c]]
        return remote(slot, slot, xg_send.at[lane, c], xg_recv.at[lane, c], "mp", target)

    if paired:
        for lane, peer in ((0, far), (1, near)):
            for c, piece in enumerate(pieces):
                send = remote(
                    x_hbm.at[piece], xg.at[me, piece],
                    xg_send.at[lane, c], xg_recv.at[lane, c], "mp", peer,
                )
                send.start()
                sends.append(send)
    else:
        for c, piece in enumerate(pieces):
            for step in range(1, n_mp):
                send = remote(
                    x_hbm.at[piece], xg.at[me, piece],
                    xg_send.at[step, c], xg_recv.at[step, c], "mp", lax.rem(me + step, n_mp),
                )
                send.start()
                sends.append(send)
    own_x.wait()
    for small in smalls:
        small.wait()

    def relay_far(c):
        if paired:
            gather(0, c, far, far).wait_recv()
            relay = gather(2, c, far, near)
            relay.start()
            sends.append(relay)

    def gathered(c):
        if paired:
            gather(1, c, near, near).wait_recv()
            gather(2, c, cross, near).wait_recv()
        else:
            for step in range(1, n_mp):
                source = lax.rem(me - step + n_mp, n_mp)
                gather(step, c, source, source).wait_recv()

    features = n_mp * part

    def normalize(c):
        piece = pieces[c]
        total = jnp.zeros((half, 1), F32)
        for j in range(n_mp):
            total = total + jnp.sum(xg[j, piece, :].astype(F32), axis=-1, keepdims=True)
        average = total / features
        square = jnp.zeros((half, 1), F32)
        for j in range(n_mp):
            off = xg[j, piece, :].astype(F32) - average
            square = square + jnp.sum(off * off, axis=-1, keepdims=True)
        inverse = lax.rsqrt(square / features + 1e-05)
        for j in range(n_mp):
            cols = pl.ds(j * part, part)
            off = xg[j, piece, :].astype(F32) - average
            normed[piece, cols] = (off * inverse * gain_ref[:, cols]).astype(BF16)

    def block(way, which, owner, c, target):
        slot = kv.at[which, owner, pieces[c]]
        return remote(
            slot, slot, kv_send.at[way, which, owner, c], kv_recv.at[which, owner, c], "seq", target
        )

    def project(which, weight, c):
        kv[which, spot, pieces[c]] = jnp.dot(
            normed[pieces[c], :], weight[...], preferred_element_type=F32
        ).astype(BF16)
        launch(which, c)

    def launch(which, c):
        @pl.when(has_right)
        def _():
            block(1, which, spot, c, spot + 1).start()

        @pl.when(has_left)
        def _():
            block(0, which, spot, c, spot - 1).start()

        if hop:

            @pl.when(ends)
            def _():
                block(2, which, spot, c, n_seq - 1 - spot).start()

    relay_far(0)
    gathered(0)
    normalize(0)
    relay_far(1)
    loads[0].wait()
    project(0, wk, 0)
    gathered(1)
    normalize(1)
    project(0, wk, 1)
    loads[1].wait()
    kv[1, spot] = jnp.dot(normed[...], wv[...], preferred_element_type=F32).astype(BF16)
    for c in range(2):
        launch(1, c)
    loads[2].wait()
    q_ref[...] = jnp.dot(normed[...], wq[...], preferred_element_type=F32).astype(BF16)

    def take(which, step, c, forward):
        before = spot - step
        after = spot + step

        @pl.when(before >= 0)
        def _():
            block(1, which, before, c, before).wait_recv()
            if forward:

                @pl.when(has_right)
                def _():
                    block(1, which, before, c, spot + 1).start()

        @pl.when(after < n_seq)
        def _():
            block(0, which, after, c, after).wait_recv()
            if forward:

                @pl.when(has_left)
                def _():
                    block(0, which, after, c, spot - 1).start()

    if hop:
        for which in range(2):
            for c in range(2):
                take(which, 1, c, True)
        for step in (2, 3):
            for c in range(2):
                take(0, step, c, False)

        def last_values():
            for step in (2, 3):
                for c in range(2):
                    take(1, step, c, False)

    else:

        def chain(i):
            for c in range(2):
                for which in range(2):
                    take(which, i + 1, c, True)

        each(n_seq - 1, chain)

        def last_values():
            pass

    if n_seq <= UNROLL_LIMIT:
        sums, chances = [], []
        for h in range(groups):
            cols = pl.ds(h * span, span)
            keys = kv[0, :, :, cols].reshape(n_seq * rows, span)
            s = lax.dot_general(
                q_ref[:, cols], keys, (((1,), (1,)), ((), ())), preferred_element_type=F32
            ) * (softness_ref[h] / math.sqrt(span))
            top = jnp.max(s, axis=-1, keepdims=True)
            w = jnp.exp(s - top)
            sums.append(jnp.sum(w, axis=-1, keepdims=True))
            chances.append(w.astype(BF16))
        last_values()
        for h in range(groups):
            cols = pl.ds(h * span, span)
            values = kv[1, :, :, cols].reshape(n_seq * rows, span)
            mixed = jnp.dot(chances[h], values, preferred_element_type=F32)
            heads[:, cols] = (mixed / sums[h]).astype(BF16)
    else:
        for h in range(groups):
            cols = pl.ds(h * span, span)
            factor = softness_ref[h] / math.sqrt(span)

            def first(b, top):
                s = lax.dot_general(
                    q_ref[:, cols], kv[0, b, :, cols], (((1,), (1,)), ((), ())),
                    preferred_element_type=F32,
                ) * factor
                scores[b] = s
                return jnp.maximum(top, jnp.max(s, axis=-1, keepdims=True))

            top = lax.fori_loop(0, n_seq, first, jnp.full((rows, 1), -jnp.inf, F32))

            def second(b, state):
                summed, mixed = state
                w = jnp.exp(scores[b] - top)
                mixed = mixed + jnp.dot(
                    w.astype(BF16), kv[1, b, :, cols], preferred_element_type=F32
                )
                return summed + jnp.sum(w, axis=-1, keepdims=True), mixed

            summed, mixed = lax.fori_loop(
                0, n_seq, second, (jnp.zeros((rows, 1), F32), jnp.zeros((rows, span), F32))
            )
            heads[:, cols] = (mixed / summed).astype(BF16)

    loads[3].wait()
    rs_pieces = [pl.ds(i * (rows // RS_PIECES), rows // RS_PIECES) for i in range(RS_PIECES)]

    def share(owner):
        cols = pl.ds(pl.multiple_of(owner * part, part), part)
        return jnp.dot(heads[...], wo[:, cols], preferred_element_type=F32)

    if paired:
        quarter = rows // len(rs_pieces)

        def reduce(lane, piece, target):
            return remote(
                out_send.at[lane, piece], out_recv.at[lane, piece],
                rs_send.at[lane, piece.start // quarter], rs_recv.at[lane, piece.start // quarter],
                "mp", target,
            )

        out_send[0] = share(cross).astype(BF16)
        for piece in rs_pieces:
            send = reduce(0, piece, near)
            send.start()
            sends.append(send)
        for_far = share(far)
        for piece in rs_pieces:
            reduce(0, piece, near).wait_recv()
            low = piece.start
            out_send[2, piece] = (
                for_far[low : low + quarter] + out_recv[0, piece].astype(F32)
            ).astype(BF16)
            send = reduce(2, piece, far)
            send.start()
            sends.append(send)
        out_send[1] = share(near).astype(BF16)
        for piece in rs_pieces:
            send = reduce(1, piece, near)
            send.start()
            sends.append(send)
        own = share(me) + xg[me].astype(F32)
        for piece in rs_pieces:
            reduce(1, piece, near).wait_recv()
        own = own + out_recv[1].astype(F32)
        for piece in rs_pieces:
            reduce(2, piece, far).wait_recv()
            low = piece.start
            out_ref[piece, :] = (
                own[low : low + quarter] + out_recv[2, piece].astype(F32)
            ).astype(BF16)
    else:
        for step in range(1, n_mp):
            peer = lax.rem(me + step, n_mp)
            out_send[step] = share(peer).astype(BF16)
            send = remote(
                out_send.at[step], out_recv.at[step], rs_send.at[step, 0], rs_recv.at[step, 0], "mp", peer
            )
            send.start()
            sends.append(send)
        own = share(me) + xg[me].astype(F32)
        for step in range(1, n_mp):
            remote(
                out_send.at[step], out_recv.at[step], rs_send.at[step, 0], rs_recv.at[step, 0], "mp", me
            ).wait_recv()
            own = own + out_recv[step].astype(F32)
        out_ref[...] = own.astype(BF16)

    for send in sends:
        send.wait_send()

    def drain(b):
        for which in range(2):
            for c in range(2):
                to_right = (b == spot) | (b == spot - 1) if hop else b <= spot
                to_left = (b == spot) | (b == spot + 1) if hop else b >= spot

                @pl.when(has_right & to_right)
                def _():
                    block(1, which, b, c, spot + 1).wait_send()

                @pl.when(has_left & to_left)
                def _():
                    block(0, which, b, c, spot - 1).wait_send()

                if hop:

                    @pl.when(ends & (b == spot))
                    def _():
                        block(2, which, b, c, n_seq - 1 - spot).wait_send()

    each(n_seq, drain)


def per_device(n_mp, n_seq, x, gain, wq, wk, wv, softness, wo):
    rows, part = x.shape
    features, head_cols = wq.shape
    span_rows = n_seq if n_seq > UNROLL_LIMIT else 1
    any_space = pl.BlockSpec(memory_space=pl.ANY)
    vmem = pl.BlockSpec(memory_space=pltpu.VMEM)
    slots = max(n_mp, 3)
    return pl.pallas_call(
        functools.partial(kernel, n_mp, n_seq),
        out_shape=pltpu.VMEM((rows, part), BF16),
        in_specs=[
            any_space, any_space, any_space, any_space, any_space, any_space, any_space,
        ],
        out_specs=vmem,
        scratch_shapes=[
            pltpu.SMEM(softness.shape, F32),
            pltpu.VMEM((1, features), F32),
            pltpu.VMEM((n_mp, rows, part), BF16),
            pltpu.VMEM((features, head_cols), BF16),
            pltpu.VMEM((features, head_cols), BF16),
            pltpu.VMEM((features, head_cols), BF16),
            pltpu.VMEM((head_cols, features), BF16),
            pltpu.VMEM((rows, features), BF16),
            pltpu.VMEM((rows, head_cols), BF16),
            pltpu.VMEM((2, n_seq, rows, head_cols), BF16),
            pltpu.VMEM((span_rows, rows, rows), F32),
            pltpu.VMEM((rows, head_cols), BF16),
            pltpu.VMEM((slots, rows, part), BF16),
            pltpu.VMEM((slots, rows, part), BF16),
            pltpu.SemaphoreType.DMA((2,)),
            pltpu.SemaphoreType.DMA((4,)),
            pltpu.SemaphoreType.DMA,
            pltpu.SemaphoreType.DMA((slots, 2)),
            pltpu.SemaphoreType.DMA((slots, 2)),
            pltpu.SemaphoreType.DMA((3, 2, n_seq, 2)),
            pltpu.SemaphoreType.DMA((2, n_seq, 2)),
            pltpu.SemaphoreType.DMA((slots, RS_PIECES)),
            pltpu.SemaphoreType.DMA((slots, RS_PIECES)),
        ],
        compiler_params=pltpu.CompilerParams(collective_id=0, has_side_effects=True),
    )(softness, x, gain.reshape(1, features), wq, wk, wv, wo)


def line_kernel(
    softness_hbm, x_hbm, gain_hbm, wq_hbm, wk_hbm, wv_hbm, wo_hbm, out_ref,
    softness_ref, gain_ref, xg, xe, wq, wkv, wo, normed, q_ref, kv, heads,
    go_sem, up_sem, small_sem, w_sem, x_sem, xg_send, xg_recv, kv_send, kv_recv,
    wo_send, wo_recv, h_send, h_recv, e_send, e_recv,
):
    n_mp, n_seq = xg.shape[0], kv.shape[0]
    me = lax.axis_index("mp")
    spot = lax.axis_index("seq")
    group = lax.axis_index("groups")
    other = 1 - group
    rows, part = x_hbm.shape
    head_cols = wq_hbm.shape[1]
    groups = softness_hbm.shape[0]
    span = head_cols // groups
    features = n_mp * part
    last = n_seq - 1
    has_left = spot > 0
    has_right = spot < last
    is_first = spot == 0
    is_last = spot == last
    at_end = is_first | is_last
    opposite = last - spot
    odd = lax.rem(me, 2)
    is_odd = odd == 1
    is_even = odd == 0
    near = me + 1 - 2 * odd
    far = lax.rem(me + 2, n_mp)
    cross = lax.rem(near + 2, n_mp)
    even_me = me - odd
    odd_me = even_me + 1

    def columns(owner):
        return pl.ds(pl.multiple_of(owner * part, part), part)

    own_x = pltpu.make_async_copy(x_hbm, xg.at[me], x_sem)
    own_x.start()

    barrier = pltpu.get_barrier_semaphore()

    def greet(**where):
        pl.semaphore_signal(barrier, inc=1, device_id=where, device_id_type=MESH)

    @pl.when(is_odd)
    def _():
        greet(mp=far)

    @pl.when(is_even)
    def _():
        greet(mp=near)
        greet(mp=cross)

    greet(groups=other, mp=odd_me)
    for plane in range(n_seq):

        @pl.when(plane > spot)
        def _():
            greet(seq=plane, mp=odd_me)

        @pl.when(plane < spot)
        def _():
            greet(seq=plane, mp=even_me)

    smalls = [
        pltpu.make_async_copy(gain_hbm, gain_ref, small_sem.at[0]),
        pltpu.make_async_copy(softness_hbm, softness_ref, small_sem.at[1]),
    ]
    for small in smalls:
        small.start()
    loads = [
        pltpu.make_async_copy(src, dst, w_sem.at[i])
        for i, (src, dst) in enumerate(
            (
                (wk_hbm, wkv.at[:, pl.ds(0, head_cols)]),
                (wv_hbm, wkv.at[:, pl.ds(head_cols, head_cols)]),
                (wq_hbm, wq),
                (wo_hbm.at[:, columns(me)], wo.at[me]),
            )
        )
    ]
    for load in loads:
        load.start()

    @pl.when(is_odd)
    def _():
        pl.semaphore_wait(barrier, n_mp - 1 + 2 + 2 * spot)
        pl.semaphore_signal(go_sem, inc=1, device_id={"mp": near}, device_id_type=MESH)

    @pl.when(is_even)
    def _():
        pl.semaphore_wait(go_sem, 1)

    piece_rows = rows // X_PIECES
    half = rows // 2
    halves = [pl.ds(0, half), pl.ds(half, half)]
    pieces = [pl.ds(c * piece_rows, piece_rows) for c in range(X_PIECES)]
    sends = []

    def gather(lane, c, source, target):
        slot = xg.at[source, pieces[c]]
        return remote(slot, slot, xg_send.at[lane, c], xg_recv.at[lane, c], "mp", target)

    for c, piece in enumerate(pieces):
        send = remote(
            x_hbm.at[piece], xg.at[me, piece],
            xg_send.at[0, c], xg_recv.at[0, c], "mp", far,
        )
        send.start()
        sends.append(send)
    send = remote(x_hbm, xg.at[me], xg_send.at[1, 0], xg_recv.at[1, 0], "mp", near)
    send.start()
    sends.append(send)
    own_x.wait()
    for small in smalls:
        small.wait()

    def relay_far(c):
        gather(0, c, far, far).wait_recv()
        relay = gather(2, c, far, near)
        relay.start()
        sends.append(relay)

    def gathered(c):
        if c == 0:
            remote(
                x_hbm, xg.at[near], xg_send.at[1, 0], xg_recv.at[1, 0], "mp", near
            ).wait_recv()
        gather(2, c, cross, near).wait_recv()

    def normalize(c, held):
        piece = pieces[c]
        total = jnp.zeros((piece_rows, 1), F32)
        for j in range(n_mp):
            total = total + jnp.sum(held[j, piece, :].astype(F32), axis=-1, keepdims=True)
        average = total / features
        square = jnp.zeros((piece_rows, 1), F32)
        for j in range(n_mp):
            off = held[j, piece, :].astype(F32) - average
            square = square + jnp.sum(off * off, axis=-1, keepdims=True)
        inverse = lax.rsqrt(square / features + 1e-05)
        for j in range(n_mp):
            cols = pl.ds(j * part, part)
            off = held[j, piece, :].astype(F32) - average
            normed[piece, cols] = (off * inverse * gain_ref[:, cols]).astype(BF16)

    def know_later_planes(when):
        @pl.when(when & is_even)
        def _():
            pl.semaphore_wait(barrier, 2 * (last - spot))
            pl.semaphore_signal(up_sem, inc=1, device_id={"mp": near}, device_id_type=MESH)

        @pl.when(when & is_odd)
        def _():
            pl.semaphore_wait(up_sem, 1)

    def end_piece(lane, c, source, target, axis="mp"):
        slot = xe.at[source, pieces[c]]
        return remote(slot, slot, e_send.at[lane, c], e_recv.at[lane, c], axis, target)

    def to_other_end(c):
        return remote(
            x_hbm.at[pieces[c]], xe.at[me, pieces[c]],
            e_send.at[3, c], e_recv.at[3, c], "seq", opposite,
        )

    def send_to_other_end(when):
        @pl.when(when)
        def _():
            for c in range(X_PIECES):
                to_other_end(c).start()

    def block(owner, c, target, lane=None):
        slot = kv.at[owner, halves[c]]
        lane = target if lane is None else lane
        return remote(slot, slot, kv_send.at[lane, c], kv_recv.at[owner, c], "seq", target)

    def project(c, owner):
        kv[owner, halves[c]] = jnp.dot(
            normed[halves[c], :], wkv[...], preferred_element_type=F32
        ).astype(BF16)

    def launch(target, c, when):
        @pl.when(when)
        def _():
            block(spot, c, target).start()

    exit_rows = head_cols // 2

    def exit_half(lane, source, rows_of, target, axis):
        there = pl.ds(pl.multiple_of(rows_of * exit_rows, exit_rows), exit_rows)
        slot = wo.at[source, there]
        return remote(slot, slot, wo_send.at[lane], wo_recv.at[lane], axis, target)

    near_exit = remote(
        wo_hbm.at[:, columns(near)], wo.at[me], wo_send.at[0], wo_recv.at[0], "mp", near
    )
    mine = pl.ds(pl.multiple_of(group * exit_rows, exit_rows), exit_rows)
    exits = [
        remote(
            wo_hbm.at[mine, columns(peer)], wo.at[me, mine],
            wo_send.at[lane], wo_recv.at[lane], "mp", peer,
        )
        for lane, peer in ((1, far), (2, cross))
    ] + [near_exit]

    send_to_other_end(is_last)
    for send in exits:
        send.start()
        sends.append(send)
    for c in range(X_PIECES):
        relay_far(c)
    know_later_planes(is_first)
    send_to_other_end(is_first)
    for c in range(X_PIECES):
        gathered(c)
        normalize(c, xg)
        done = (c + 1) * piece_rows
        if done == half:
            loads[0].wait()
            loads[1].wait()
            project(0, spot)
            launch(0, 0, spot == 1)
            launch(1, 0, spot == 2)
    project(1, spot)
    launch(0, 1, spot == 1)
    launch(1, 1, spot == 2)
    know_later_planes(has_left & has_right)
    for c in range(2):
        launch(last, c, spot == last - 1)
    for target in range(1, last):
        for c in range(2):
            launch(target, c, spot < target)
    for target in range(last - 1, 0, -1):
        for c in range(2):
            launch(target, c, spot == last)

    loads[2].wait()
    q_ref[...] = jnp.dot(normed[...], wq[...], preferred_element_type=F32).astype(BF16)

    def weigh(queries, keys, h):
        s = lax.dot_general(
            queries, keys, (((1,), (1,)), ((), ())), preferred_element_type=F32
        ) * (softness_ref[h] / math.sqrt(span))
        top = jnp.max(s, axis=-1, keepdims=True)
        w = jnp.exp(s - top)
        return jnp.sum(w, axis=-1, keepdims=True), w.astype(BF16)

    head = [pl.ds(h * span, span) for h in range(groups)]
    passes_up = spot == last - 1
    passes_down = spot == 1

    def exchanged(b):
        ends = (0, last)
        return (spot != b) & (spot != last - b) if b in ends else spot != b

    def take_blocks():
        for owner in range(n_seq):
            seen = passes_up if owner == last - 2 else passes_down if owner == 2 else False

            @pl.when(exchanged(owner) & jnp.logical_not(seen))
            def _():
                for c in range(2):
                    block(owner, c, owner).wait_recv()

    def pass_exit(lane, source):
        exit_half(lane, source, group, source, "mp").wait_recv()
        send = exit_half(lane + 2, source, group, other, "groups")
        send.start()
        sends.append(send)

    @pl.when(at_end)
    def _():
        for c in range(X_PIECES):
            to_other_end(c).wait_recv()
            end_piece(0, c, me, far).start()
            end_piece(1, c, me, near).start()

    pass_exit(1, far)

    @pl.when(at_end)
    def _():
        for c in range(X_PIECES):
            end_piece(0, c, far, far).wait_recv()
            end_piece(2, c, far, near).start()

    pass_exit(2, cross)

    @pl.when(passes_up)
    def _():
        for c in range(2):
            block(last - 2, c, last - 2).wait_recv()
            block(last - 2, c, last, last - 1).start()

    @pl.when(passes_down)
    def _():
        for c in range(2):
            block(2, c, 2).wait_recv()
            block(2, c, 0, 1).start()

    @pl.when(at_end)
    def _():
        for c in range(X_PIECES):
            end_piece(1, c, near, near).wait_recv()
            end_piece(2, c, cross, near).wait_recv()
            normalize(c, xe)
            done = (c + 1) * piece_rows
            if done % half == 0:
                project(done // half - 1, opposite)

    def share(lane, h, source, target):
        slot = heads.at[source, :, head[h]]
        return remote(slot, slot, h_send.at[lane, h], h_recv.at[lane, h], "mp", target)

    even_peer = lax.rem(even_me + 2, n_mp)
    odd_peer = even_peer + 1

    def give(h, mixed):
        heads[me, :, head[h]] = mixed.astype(BF16)
        share(odd, h, me, even_peer).start()

    take_blocks()
    known = []
    for h in range(groups):
        keys = kv[:, :, head[h]].reshape(n_seq * rows, span)
        known.append(weigh(q_ref[:, head[h]], keys, h))
    for h in range(groups):
        values = kv[:, :, pl.ds(head_cols + h * span, span)].reshape(n_seq * rows, span)
        summed, w = known[h]
        give(h, jnp.dot(w, values, preferred_element_type=F32) / summed)

    for h in range(groups):
        sends.append(share(odd, h, me, even_peer))
        for lane, target in ((1 - odd, odd_peer), (2, near)):
            send = share(lane, h, me, target)
            send.start()
            sends.append(send)

    loads[3].wait()
    total = xg[me].astype(F32) + jnp.dot(heads[me], wo[me], preferred_element_type=F32)
    near_exit.wait_recv()
    for lane, source in ((1, far), (2, cross)):
        exit_half(lane + 2, source, other, other, "groups").wait_recv()
    for lane, source in ((2, near), (0, far), (1, cross)):
        for h in range(groups):
            share(lane, h, source, source).wait_recv()
        total = total + jnp.dot(heads[source], wo[source], preferred_element_type=F32)
    out_ref[...] = total.astype(BF16)

    for send in sends:
        send.wait_send()

    for target in range(n_seq):

        by_relay = spot == last - 2 if target == last else spot == 2 if target == 0 else False

        @pl.when(exchanged(target) & jnp.logical_not(by_relay))
        def _():
            for c in range(2):
                block(spot, c, target).wait_send()

    @pl.when(passes_up)
    def _():
        for c in range(2):
            block(last - 2, c, last, last - 1).wait_send()

    @pl.when(passes_down)
    def _():
        for c in range(2):
            block(2, c, 0, 1).wait_send()

    @pl.when(at_end)
    def _():
        for c in range(X_PIECES):
            to_other_end(c).wait_send()
            end_piece(0, c, me, far).wait_send()
            end_piece(1, c, me, near).wait_send()
            end_piece(2, c, far, near).wait_send()


def line_call(n_mp, n_seq, x, gain, wq, wk, wv, softness, wo):
    rows, part = x.shape
    features, head_cols = wq.shape
    heads = softness.shape[0]
    any_space = pl.BlockSpec(memory_space=pl.ANY)
    return pl.pallas_call(
        line_kernel,
        out_shape=pltpu.VMEM((rows, part), BF16),
        in_specs=[any_space] * 7,
        out_specs=pl.BlockSpec(memory_space=pltpu.VMEM),
        scratch_shapes=[
            pltpu.SMEM(softness.shape, F32),
            pltpu.VMEM((1, features), F32),
            pltpu.VMEM((n_mp, rows, part), BF16),
            pltpu.VMEM((n_mp, rows, part), BF16),
            pltpu.VMEM((features, head_cols), BF16),
            pltpu.VMEM((features, 2 * head_cols), BF16),
            pltpu.VMEM((n_mp, head_cols, part), BF16),
            pltpu.VMEM((rows, features), BF16),
            pltpu.VMEM((rows, head_cols), BF16),
            pltpu.VMEM((n_seq, rows, 2 * head_cols), BF16),
            pltpu.VMEM((n_mp, rows, head_cols), BF16),
            pltpu.SemaphoreType.REGULAR,
            pltpu.SemaphoreType.REGULAR,
            pltpu.SemaphoreType.DMA((2,)),
            pltpu.SemaphoreType.DMA((4,)),
            pltpu.SemaphoreType.DMA,
            pltpu.SemaphoreType.DMA((3, X_PIECES)),
            pltpu.SemaphoreType.DMA((3, X_PIECES)),
            pltpu.SemaphoreType.DMA((n_seq, 2)),
            pltpu.SemaphoreType.DMA((n_seq, 2)),
            pltpu.SemaphoreType.DMA((5,)),
            pltpu.SemaphoreType.DMA((5,)),
            pltpu.SemaphoreType.DMA((3, heads)),
            pltpu.SemaphoreType.DMA((3, heads)),
            pltpu.SemaphoreType.DMA((4, X_PIECES)),
            pltpu.SemaphoreType.DMA((4, X_PIECES)),
        ],
        compiler_params=pltpu.CompilerParams(
            collective_id=0, has_side_effects=True, vmem_limit_bytes=VMEM_BYTES
        ),
    )(softness, x, gain.reshape(1, features), wq, wk, wv, wo)


def solution(mesh):
    short = mesh.shape["mp"] == 4 and mesh.shape["seq"] == 4 and mesh.shape["groups"] == 2
    return jax.shard_map(
        functools.partial(line_call if short else per_device, mesh.shape["mp"], mesh.shape["seq"]),
        mesh=mesh,
        in_specs=(
            P(("groups", "seq"), "mp"),
            P(),
            P(None, "mp"),
            P(None, "mp"),
            P(None, "mp"),
            P("mp"),
            P("mp", None),
        ),
        out_specs=P(("groups", "seq"), "mp"),
        check_vma=False,
    )
```

```python
import functools
import math

import jax
import jax.numpy as jnp
from jax import lax
from jax.experimental import pallas as pl
from jax.experimental.pallas import tpu as pltpu
from jax.sharding import PartitionSpec as P

MESH = pl.DeviceIdType.MESH
F32 = jnp.float32
BF16 = jnp.bfloat16
UNROLL_LIMIT = 8
RS_PIECES = 2
X_PIECES = 2
VMEM_BYTES = 60 * 1024 * 1024


def remote(src, dst, send_sem, recv_sem, axis, index):
    return pltpu.make_async_remote_copy(
        src_ref=src,
        dst_ref=dst,
        send_sem=send_sem,
        recv_sem=recv_sem,
        device_id={axis: index},
        device_id_type=MESH,
    )


def each(count, body):
    if count <= UNROLL_LIMIT:
        for i in range(count):
            body(i)
    else:
        lax.fori_loop(0, count, lambda i, c: (body(i), c)[1], 0)


def kernel(
    n_mp,
    n_seq,
    softness_hbm,
    x_hbm,
    gain_hbm,
    wq_hbm,
    wk_hbm,
    wv_hbm,
    wo_hbm,
    out_ref,
    softness_ref,
    gain_ref,
    xg,
    wq,
    wk,
    wv,
    wo,
    normed,
    q_ref,
    kv,
    scores,
    heads,
    out_send,
    out_recv,
    small_sem,
    w_sem,
    x_sem,
    xg_send,
    xg_recv,
    kv_send,
    kv_recv,
    rs_send,
    rs_recv,
):
    me = lax.axis_index("mp")
    spot = lax.axis_index("seq")
    rows, part = x_hbm.shape
    head_cols = wq_hbm.shape[1]
    groups = softness_hbm.shape[0]
    span = head_cols // groups
    paired = n_mp == 4
    has_left = spot > 0
    has_right = spot < n_seq - 1
    hop = n_seq == 4
    ends = (spot == 0) | (spot == n_seq - 1)

    own_x = pltpu.make_async_copy(x_hbm, xg.at[me], x_sem)
    own_x.start()
    smalls = [
        pltpu.make_async_copy(gain_hbm, gain_ref, small_sem.at[0]),
        pltpu.make_async_copy(softness_hbm, softness_ref, small_sem.at[1]),
    ]
    for small in smalls:
        small.start()
    loads = [
        pltpu.make_async_copy(src, dst, w_sem.at[i])
        for i, (src, dst) in enumerate(((wk_hbm, wk), (wv_hbm, wv), (wq_hbm, wq), (wo_hbm, wo)))
    ]
    for load in loads:
        load.start()

    barrier = pltpu.get_barrier_semaphore()
    for step in range(1, n_mp):
        pl.semaphore_signal(
            barrier, inc=1, device_id={"mp": lax.rem(me + step, n_mp)}, device_id_type=MESH
        )

    @pl.when(has_left)
    def _():
        pl.semaphore_signal(barrier, inc=1, device_id={"seq": spot - 1}, device_id_type=MESH)

    @pl.when(has_right)
    def _():
        pl.semaphore_signal(barrier, inc=1, device_id={"seq": spot + 1}, device_id_type=MESH)

    greeted = n_mp - 1 + has_left.astype(jnp.int32) + has_right.astype(jnp.int32)
    if hop:

        @pl.when(ends)
        def _():
            pl.semaphore_signal(
                barrier, inc=1, device_id={"seq": n_seq - 1 - spot}, device_id_type=MESH
            )

        greeted = greeted + ends.astype(jnp.int32)
    pl.semaphore_wait(barrier, greeted)

    half = rows // 2
    pieces = [pl.ds(0, half), pl.ds(half, half)]
    near = me + 1 - 2 * lax.rem(me, 2)
    far = lax.rem(me + 2, n_mp)
    cross = lax.rem(near + 2, n_mp)
    sends = []

    def gather(lane, c, source, target):
        slot = xg.at[source, pieces[c]]
        return remote(slot, slot, xg_send.at[lane, c], xg_recv.at[lane, c], "mp", target)

    if paired:
        for lane, peer in ((0, far), (1, near)):
            for c, piece in enumerate(pieces):
                send = remote(
                    x_hbm.at[piece], xg.at[me, piece],
                    xg_send.at[lane, c], xg_recv.at[lane, c], "mp", peer,
                )
                send.start()
                sends.append(send)
    else:
        for c, piece in enumerate(pieces):
            for step in range(1, n_mp):
                send = remote(
                    x_hbm.at[piece], xg.at[me, piece],
                    xg_send.at[step, c], xg_recv.at[step, c], "mp", lax.rem(me + step, n_mp),
                )
                send.start()
                sends.append(send)
    own_x.wait()
    for small in smalls:
        small.wait()

    def relay_far(c):
        if paired:
            gather(0, c, far, far).wait_recv()
            relay = gather(2, c, far, near)
            relay.start()
            sends.append(relay)

    def gathered(c):
        if paired:
            gather(1, c, near, near).wait_recv()
            gather(2, c, cross, near).wait_recv()
        else:
            for step in range(1, n_mp):
                source = lax.rem(me - step + n_mp, n_mp)
                gather(step, c, source, source).wait_recv()

    features = n_mp * part

    def normalize(c):
        piece = pieces[c]
        total = jnp.zeros((half, 1), F32)
        for j in range(n_mp):
            total = total + jnp.sum(xg[j, piece, :].astype(F32), axis=-1, keepdims=True)
        average = total / features
        square = jnp.zeros((half, 1), F32)
        for j in range(n_mp):
            off = xg[j, piece, :].astype(F32) - average
            square = square + jnp.sum(off * off, axis=-1, keepdims=True)
        inverse = lax.rsqrt(square / features + 1e-05)
        for j in range(n_mp):
            cols = pl.ds(j * part, part)
            off = xg[j, piece, :].astype(F32) - average
            normed[piece, cols] = (off * inverse * gain_ref[:, cols]).astype(BF16)

    def block(way, which, owner, c, target):
        slot = kv.at[which, owner, pieces[c]]
        return remote(
            slot, slot, kv_send.at[way, which, owner, c], kv_recv.at[which, owner, c], "seq", target
        )

    def project(which, weight, c):
        kv[which, spot, pieces[c]] = jnp.dot(
            normed[pieces[c], :], weight[...], preferred_element_type=F32
        ).astype(BF16)
        launch(which, c)

    def launch(which, c):
        @pl.when(has_right)
        def _():
            block(1, which, spot, c, spot + 1).start()

        @pl.when(has_left)
        def _():
            block(0, which, spot, c, spot - 1).start()

        if hop:

            @pl.when(ends)
            def _():
                block(2, which, spot, c, n_seq - 1 - spot).start()

    relay_far(0)
    gathered(0)
    normalize(0)
    relay_far(1)
    loads[0].wait()
    project(0, wk, 0)
    gathered(1)
    normalize(1)
    project(0, wk, 1)
    loads[1].wait()
    kv[1, spot] = jnp.dot(normed[...], wv[...], preferred_element_type=F32).astype(BF16)
    for c in range(2):
        launch(1, c)
    loads[2].wait()
    q_ref[...] = jnp.dot(normed[...], wq[...], preferred_element_type=F32).astype(BF16)

    def take(which, step, c, forward):
        before = spot - step
        after = spot + step

        @pl.when(before >= 0)
        def _():
            block(1, which, before, c, before).wait_recv()
            if forward:

                @pl.when(has_right)
                def _():
                    block(1, which, before, c, spot + 1).start()

        @pl.when(after < n_seq)
        def _():
            block(0, which, after, c, after).wait_recv()
            if forward:

                @pl.when(has_left)
                def _():
                    block(0, which, after, c, spot - 1).start()

    if hop:
        for which in range(2):
            for c in range(2):
                take(which, 1, c, True)
        for step in (2, 3):
            for c in range(2):
                take(0, step, c, False)

        def last_values():
            for step in (2, 3):
                for c in range(2):
                    take(1, step, c, False)

    else:

        def chain(i):
            for c in range(2):
                for which in range(2):
                    take(which, i + 1, c, True)

        each(n_seq - 1, chain)

        def last_values():
            pass

    if n_seq <= UNROLL_LIMIT:
        sums, chances = [], []
        for h in range(groups):
            cols = pl.ds(h * span, span)
            keys = kv[0, :, :, cols].reshape(n_seq * rows, span)
            s = lax.dot_general(
                q_ref[:, cols], keys, (((1,), (1,)), ((), ())), preferred_element_type=F32
            ) * (softness_ref[h] / math.sqrt(span))
            top = jnp.max(s, axis=-1, keepdims=True)
            w = jnp.exp(s - top)
            sums.append(jnp.sum(w, axis=-1, keepdims=True))
            chances.append(w.astype(BF16))
        last_values()
        for h in range(groups):
            cols = pl.ds(h * span, span)
            values = kv[1, :, :, cols].reshape(n_seq * rows, span)
            mixed = jnp.dot(chances[h], values, preferred_element_type=F32)
            heads[:, cols] = (mixed / sums[h]).astype(BF16)
    else:
        for h in range(groups):
            cols = pl.ds(h * span, span)
            factor = softness_ref[h] / math.sqrt(span)

            def first(b, top):
                s = lax.dot_general(
                    q_ref[:, cols], kv[0, b, :, cols], (((1,), (1,)), ((), ())),
                    preferred_element_type=F32,
                ) * factor
                scores[b] = s
                return jnp.maximum(top, jnp.max(s, axis=-1, keepdims=True))

            top = lax.fori_loop(0, n_seq, first, jnp.full((rows, 1), -jnp.inf, F32))

            def second(b, state):
                summed, mixed = state
                w = jnp.exp(scores[b] - top)
                mixed = mixed + jnp.dot(
                    w.astype(BF16), kv[1, b, :, cols], preferred_element_type=F32
                )
                return summed + jnp.sum(w, axis=-1, keepdims=True), mixed

            summed, mixed = lax.fori_loop(
                0, n_seq, second, (jnp.zeros((rows, 1), F32), jnp.zeros((rows, span), F32))
            )
            heads[:, cols] = (mixed / summed).astype(BF16)

    loads[3].wait()
    rs_pieces = [pl.ds(i * (rows // RS_PIECES), rows // RS_PIECES) for i in range(RS_PIECES)]

    def share(owner):
        cols = pl.ds(pl.multiple_of(owner * part, part), part)
        return jnp.dot(heads[...], wo[:, cols], preferred_element_type=F32)

    if paired:
        quarter = rows // len(rs_pieces)

        def reduce(lane, piece, target):
            return remote(
                out_send.at[lane, piece], out_recv.at[lane, piece],
                rs_send.at[lane, piece.start // quarter], rs_recv.at[lane, piece.start // quarter],
                "mp", target,
            )

        out_send[0] = share(cross).astype(BF16)
        for piece in rs_pieces:
            send = reduce(0, piece, near)
            send.start()
            sends.append(send)
        for_far = share(far)
        for piece in rs_pieces:
            reduce(0, piece, near).wait_recv()
            low = piece.start
            out_send[2, piece] = (
                for_far[low : low + quarter] + out_recv[0, piece].astype(F32)
            ).astype(BF16)
            send = reduce(2, piece, far)
            send.start()
            sends.append(send)
        out_send[1] = share(near).astype(BF16)
        for piece in rs_pieces:
            send = reduce(1, piece, near)
            send.start()
            sends.append(send)
        own = share(me) + xg[me].astype(F32)
        for piece in rs_pieces:
            reduce(1, piece, near).wait_recv()
        own = own + out_recv[1].astype(F32)
        for piece in rs_pieces:
            reduce(2, piece, far).wait_recv()
            low = piece.start
            out_ref[piece, :] = (
                own[low : low + quarter] + out_recv[2, piece].astype(F32)
            ).astype(BF16)
    else:
        for step in range(1, n_mp):
            peer = lax.rem(me + step, n_mp)
            out_send[step] = share(peer).astype(BF16)
            send = remote(
                out_send.at[step], out_recv.at[step], rs_send.at[step, 0], rs_recv.at[step, 0], "mp", peer
            )
            send.start()
            sends.append(send)
        own = share(me) + xg[me].astype(F32)
        for step in range(1, n_mp):
            remote(
                out_send.at[step], out_recv.at[step], rs_send.at[step, 0], rs_recv.at[step, 0], "mp", me
            ).wait_recv()
            own = own + out_recv[step].astype(F32)
        out_ref[...] = own.astype(BF16)

    for send in sends:
        send.wait_send()

    def drain(b):
        for which in range(2):
            for c in range(2):
                to_right = (b == spot) | (b == spot - 1) if hop else b <= spot
                to_left = (b == spot) | (b == spot + 1) if hop else b >= spot

                @pl.when(has_right & to_right)
                def _():
                    block(1, which, b, c, spot + 1).wait_send()

                @pl.when(has_left & to_left)
                def _():
                    block(0, which, b, c, spot - 1).wait_send()

                if hop:

                    @pl.when(ends & (b == spot))
                    def _():
                        block(2, which, b, c, n_seq - 1 - spot).wait_send()

    each(n_seq, drain)


def per_device(n_mp, n_seq, x, gain, wq, wk, wv, softness, wo):
    rows, part = x.shape
    features, head_cols = wq.shape
    span_rows = n_seq if n_seq > UNROLL_LIMIT else 1
    any_space = pl.BlockSpec(memory_space=pl.ANY)
    vmem = pl.BlockSpec(memory_space=pltpu.VMEM)
    slots = max(n_mp, 3)
    return pl.pallas_call(
        functools.partial(kernel, n_mp, n_seq),
        out_shape=pltpu.VMEM((rows, part), BF16),
        in_specs=[
            any_space, any_space, any_space, any_space, any_space, any_space, any_space,
        ],
        out_specs=vmem,
        scratch_shapes=[
            pltpu.SMEM(softness.shape, F32),
            pltpu.VMEM((1, features), F32),
            pltpu.VMEM((n_mp, rows, part), BF16),
            pltpu.VMEM((features, head_cols), BF16),
            pltpu.VMEM((features, head_cols), BF16),
            pltpu.VMEM((features, head_cols), BF16),
            pltpu.VMEM((head_cols, features), BF16),
            pltpu.VMEM((rows, features), BF16),
            pltpu.VMEM((rows, head_cols), BF16),
            pltpu.VMEM((2, n_seq, rows, head_cols), BF16),
            pltpu.VMEM((span_rows, rows, rows), F32),
            pltpu.VMEM((rows, head_cols), BF16),
            pltpu.VMEM((slots, rows, part), BF16),
            pltpu.VMEM((slots, rows, part), BF16),
            pltpu.SemaphoreType.DMA((2,)),
            pltpu.SemaphoreType.DMA((4,)),
            pltpu.SemaphoreType.DMA,
            pltpu.SemaphoreType.DMA((slots, 2)),
            pltpu.SemaphoreType.DMA((slots, 2)),
            pltpu.SemaphoreType.DMA((3, 2, n_seq, 2)),
            pltpu.SemaphoreType.DMA((2, n_seq, 2)),
            pltpu.SemaphoreType.DMA((slots, RS_PIECES)),
            pltpu.SemaphoreType.DMA((slots, RS_PIECES)),
        ],
        compiler_params=pltpu.CompilerParams(collective_id=0, has_side_effects=True),
    )(softness, x, gain.reshape(1, features), wq, wk, wv, wo)


def line_kernel(
    softness_hbm, x_hbm, gain_hbm, wq_hbm, wk_hbm, wv_hbm, wo_hbm, out_ref,
    softness_ref, gain_ref, xg, xe, wq, wkv, wo, normed, q_ref, kv, heads,
    go_sem, up_sem, small_sem, w_sem, x_sem, xg_send, xg_recv, kv_send, kv_recv,
    wo_send, wo_recv, h_send, h_recv, e_send, e_recv,
):
    n_mp, n_seq = xg.shape[0], kv.shape[0]
    me = lax.axis_index("mp")
    spot = lax.axis_index("seq")
    group = lax.axis_index("groups")
    other = 1 - group
    rows, part = x_hbm.shape
    head_cols = wq_hbm.shape[1]
    groups = softness_hbm.shape[0]
    span = head_cols // groups
    features = n_mp * part
    last = n_seq - 1
    has_left = spot > 0
    has_right = spot < last
    is_first = spot == 0
    is_last = spot == last
    at_end = is_first | is_last
    opposite = last - spot
    odd = lax.rem(me, 2)
    is_odd = odd == 1
    is_even = odd == 0
    near = me + 1 - 2 * odd
    far = lax.rem(me + 2, n_mp)
    cross = lax.rem(near + 2, n_mp)
    even_me = me - odd
    odd_me = even_me + 1

    def columns(owner):
        return pl.ds(pl.multiple_of(owner * part, part), part)

    own_x = pltpu.make_async_copy(x_hbm, xg.at[me], x_sem)
    own_x.start()

    barrier = pltpu.get_barrier_semaphore()

    def greet(**where):
        pl.semaphore_signal(barrier, inc=1, device_id=where, device_id_type=MESH)

    leader = jnp.where(is_last, me, odd_me)

    @pl.when(is_odd | is_last)
    def _():
        greet(mp=far)

    @pl.when(is_even | is_last)
    def _():
        greet(mp=near)
        greet(mp=cross)

    greet(groups=other, mp=leader)
    for plane in range(n_seq):

        @pl.when(plane > spot)
        def _():
            greet(seq=plane, mp=me if plane == last else odd_me)

        @pl.when(plane < spot)
        def _():
            greet(seq=plane, mp=even_me)

    smalls = [
        pltpu.make_async_copy(gain_hbm, gain_ref, small_sem.at[0]),
        pltpu.make_async_copy(softness_hbm, softness_ref, small_sem.at[1]),
    ]
    for small in smalls:
        small.start()
    loads = [
        pltpu.make_async_copy(src, dst, w_sem.at[i])
        for i, (src, dst) in enumerate(
            (
                (wk_hbm, wkv.at[:, pl.ds(0, head_cols)]),
                (wv_hbm, wkv.at[:, pl.ds(head_cols, head_cols)]),
                (wq_hbm, wq),
                (wo_hbm.at[:, columns(me)], wo.at[me]),
            )
        )
    ]
    for load in loads:
        load.start()

    @pl.when(is_last)
    def _():
        pl.semaphore_wait(barrier, n_mp + spot)

    @pl.when(is_odd & has_right)
    def _():
        pl.semaphore_wait(barrier, n_mp - 1 + 2 + 2 * spot)
        pl.semaphore_signal(go_sem, inc=1, device_id={"mp": near}, device_id_type=MESH)

    @pl.when(is_even & has_right)
    def _():
        pl.semaphore_wait(go_sem, 1)

    piece_rows = rows // X_PIECES
    half = rows // 2
    halves = [pl.ds(0, half), pl.ds(half, half)]
    pieces = [pl.ds(c * piece_rows, piece_rows) for c in range(X_PIECES)]
    sends = []

    def gather(lane, c, source, target):
        slot = xg.at[source, pieces[c]]
        return remote(slot, slot, xg_send.at[lane, c], xg_recv.at[lane, c], "mp", target)

    for c, piece in enumerate(pieces):
        send = remote(
            x_hbm.at[piece], xg.at[me, piece],
            xg_send.at[0, c], xg_recv.at[0, c], "mp", far,
        )
        send.start()
        sends.append(send)
    def end_piece(lane, c, source, target, axis="mp"):
        slot = xe.at[source, pieces[c]]
        return remote(slot, slot, e_send.at[lane, c], e_recv.at[lane, c], axis, target)

    def to_other_end(c):
        return remote(
            x_hbm.at[pieces[c]], xe.at[me, pieces[c]],
            e_send.at[3, c], e_recv.at[3, c], "seq", opposite,
        )

    def send_to_other_end(when):
        @pl.when(when)
        def _():
            for c in range(X_PIECES):
                to_other_end(c).start()

    send_to_other_end(is_last)
    send = remote(x_hbm, xg.at[me], xg_send.at[1, 0], xg_recv.at[1, 0], "mp", near)
    send.start()
    sends.append(send)
    own_x.wait()
    for small in smalls:
        small.wait()

    def relay_far(c):
        gather(0, c, far, far).wait_recv()
        relay = gather(2, c, far, near)
        relay.start()
        sends.append(relay)

    def gathered(c):
        if c == 0:
            remote(
                x_hbm, xg.at[near], xg_send.at[1, 0], xg_recv.at[1, 0], "mp", near
            ).wait_recv()
        gather(2, c, cross, near).wait_recv()

    def normalize(c, held):
        piece = pieces[c]
        total = jnp.zeros((piece_rows, 1), F32)
        for j in range(n_mp):
            total = total + jnp.sum(held[j, piece, :].astype(F32), axis=-1, keepdims=True)
        average = total / features
        square = jnp.zeros((piece_rows, 1), F32)
        for j in range(n_mp):
            off = held[j, piece, :].astype(F32) - average
            square = square + jnp.sum(off * off, axis=-1, keepdims=True)
        inverse = lax.rsqrt(square / features + 1e-05)
        for j in range(n_mp):
            cols = pl.ds(j * part, part)
            off = held[j, piece, :].astype(F32) - average
            normed[piece, cols] = (off * inverse * gain_ref[:, cols]).astype(BF16)

    def know_later_planes(when):
        @pl.when(when & is_even)
        def _():
            pl.semaphore_wait(barrier, 2 * (last - spot))
            pl.semaphore_signal(up_sem, inc=1, device_id={"mp": near}, device_id_type=MESH)

        @pl.when(when & is_odd)
        def _():
            pl.semaphore_wait(up_sem, 1)

    def block(owner, c, target, lane=None):
        slot = kv.at[owner, halves[c]]
        lane = target if lane is None else lane
        return remote(slot, slot, kv_send.at[lane, c], kv_recv.at[owner, c], "seq", target)

    def project(c, owner):
        kv[owner, halves[c]] = jnp.dot(
            normed[halves[c], :], wkv[...], preferred_element_type=F32
        ).astype(BF16)

    def launch(target, c, when):
        @pl.when(when)
        def _():
            block(spot, c, target).start()

    exit_rows = head_cols // 2

    def exit_half(lane, source, rows_of, target, axis):
        there = pl.ds(pl.multiple_of(rows_of * exit_rows, exit_rows), exit_rows)
        slot = wo.at[source, there]
        return remote(slot, slot, wo_send.at[lane], wo_recv.at[lane], axis, target)

    near_exit = remote(
        wo_hbm.at[:, columns(near)], wo.at[me], wo_send.at[0], wo_recv.at[0], "mp", near
    )
    mine = pl.ds(pl.multiple_of(group * exit_rows, exit_rows), exit_rows)
    exits = [
        remote(
            wo_hbm.at[mine, columns(peer)], wo.at[me, mine],
            wo_send.at[lane], wo_recv.at[lane], "mp", peer,
        )
        for lane, peer in ((1, far), (2, cross))
    ] + [near_exit]

    for send in exits:
        send.start()
        sends.append(send)
    for c in range(X_PIECES):
        relay_far(c)
    know_later_planes(is_first)
    send_to_other_end(is_first)
    for c in range(X_PIECES):
        gathered(c)
        normalize(c, xg)
        done = (c + 1) * piece_rows
        if done == half:
            loads[0].wait()
            loads[1].wait()
            project(0, spot)
            launch(0, 0, spot == 1)
            launch(1, 0, spot == 2)
    project(1, spot)
    launch(0, 1, spot == 1)
    launch(1, 1, spot == 2)
    know_later_planes(has_left & has_right)
    for c in range(2):
        launch(last, c, spot == last - 1)
    for target in range(1, last):
        for c in range(2):
            launch(target, c, spot < target)
    for target in range(last - 1, 0, -1):
        for c in range(2):
            launch(target, c, spot == last)

    loads[2].wait()
    q_ref[...] = jnp.dot(normed[...], wq[...], preferred_element_type=F32).astype(BF16)

    def weigh(queries, keys, h):
        s = lax.dot_general(
            queries, keys, (((1,), (1,)), ((), ())), preferred_element_type=F32
        ) * (softness_ref[h] / math.sqrt(span))
        top = jnp.max(s, axis=-1, keepdims=True)
        w = jnp.exp(s - top)
        return jnp.sum(w, axis=-1, keepdims=True), w.astype(BF16)

    head = [pl.ds(h * span, span) for h in range(groups)]
    passes_up = spot == last - 1
    passes_down = spot == 1

    def exchanged(b):
        ends = (0, last)
        return (spot != b) & (spot != last - b) if b in ends else spot != b

    def take_blocks():
        for owner in range(n_seq):
            seen = passes_up if owner == last - 2 else passes_down if owner == 2 else False

            @pl.when(exchanged(owner) & jnp.logical_not(seen))
            def _():
                for c in range(2):
                    block(owner, c, owner).wait_recv()

    def pass_exit(lane, source):
        exit_half(lane, source, group, source, "mp").wait_recv()
        send = exit_half(lane + 2, source, group, other, "groups")
        send.start()
        sends.append(send)

    pass_exit(1, far)

    @pl.when(at_end)
    def _():
        for c in range(X_PIECES):
            to_other_end(c).wait_recv()
            end_piece(0, c, me, far).start()
            end_piece(1, c, me, near).start()


    pass_exit(2, cross)

    @pl.when(at_end)
    def _():
        for c in range(X_PIECES):
            end_piece(0, c, far, far).wait_recv()
            end_piece(2, c, far, near).start()


    @pl.when(passes_up)
    def _():
        for c in range(2):
            block(last - 2, c, last - 2).wait_recv()
            block(last - 2, c, last, last - 1).start()

    @pl.when(passes_down)
    def _():
        for c in range(2):
            block(2, c, 2).wait_recv()
            block(2, c, 0, 1).start()

    @pl.when(at_end)
    def _():
        for c in range(X_PIECES):
            end_piece(1, c, near, near).wait_recv()
            end_piece(2, c, cross, near).wait_recv()
            normalize(c, xe)
            done = (c + 1) * piece_rows
            if done % half == 0:
                project(done // half - 1, opposite)

    def share(lane, h, source, target):
        slot = heads.at[source, :, head[h]]
        return remote(slot, slot, h_send.at[lane, h], h_recv.at[lane, h], "mp", target)

    def give(h, mixed):
        heads[me, :, head[h]] = mixed.astype(BF16)
        share(0, h, me, far).start()

    take_blocks()
    known = []
    for h in range(groups):
        keys = kv[:, :, head[h]].reshape(n_seq * rows, span)
        known.append(weigh(q_ref[:, head[h]], keys, h))
    for h in range(groups):
        values = kv[:, :, pl.ds(head_cols + h * span, span)].reshape(n_seq * rows, span)
        summed, w = known[h]
        give(h, jnp.dot(w, values, preferred_element_type=F32) / summed)

    gifts = []
    for h in range(groups):
        gifts += [share(0, h, me, far), share(1, h, me, cross)]
        send = share(2, h, me, near)
        send.start()
        gifts.append(send)

    @pl.when(is_even)
    def _():
        for h in range(groups):
            share(1, h, me, cross).start()

    loads[3].wait()
    total = xg[me].astype(F32) + jnp.dot(heads[me], wo[me], preferred_element_type=F32)
    for send in sends:
        send.wait_send()

    for target in range(n_seq):

        by_relay = spot == last - 2 if target == last else spot == 2 if target == 0 else False

        @pl.when(exchanged(target) & jnp.logical_not(by_relay))
        def _():
            for c in range(2):
                block(spot, c, target).wait_send()

    @pl.when(passes_up)
    def _():
        for c in range(2):
            block(last - 2, c, last, last - 1).wait_send()

    @pl.when(passes_down)
    def _():
        for c in range(2):
            block(2, c, 0, 1).wait_send()

    @pl.when(at_end)
    def _():
        for c in range(X_PIECES):
            to_other_end(c).wait_send()
            end_piece(0, c, me, far).wait_send()
            end_piece(1, c, me, near).wait_send()
            end_piece(2, c, far, near).wait_send()

    near_exit.wait_recv()
    for lane, source in ((1, far), (2, cross)):
        exit_half(lane + 2, source, other, other, "groups").wait_recv()
    for lane, source in ((2, near), (0, far), (1, cross)):
        for h in range(groups):
            share(lane, h, source, source).wait_recv()
            if lane == 0:

                @pl.when(is_odd)
                def _():
                    share(1, h, source, near).start()

        total = total + jnp.dot(heads[source], wo[source], preferred_element_type=F32)
    out_ref[...] = total.astype(BF16)

    for send in gifts:
        send.wait_send()


def line_call(n_mp, n_seq, x, gain, wq, wk, wv, softness, wo):
    rows, part = x.shape
    features, head_cols = wq.shape
    heads = softness.shape[0]
    any_space = pl.BlockSpec(memory_space=pl.ANY)
    return pl.pallas_call(
        line_kernel,
        out_shape=pltpu.VMEM((rows, part), BF16),
        in_specs=[any_space] * 7,
        out_specs=pl.BlockSpec(memory_space=pltpu.VMEM),
        scratch_shapes=[
            pltpu.SMEM(softness.shape, F32),
            pltpu.VMEM((1, features), F32),
            pltpu.VMEM((n_mp, rows, part), BF16),
            pltpu.VMEM((n_mp, rows, part), BF16),
            pltpu.VMEM((features, head_cols), BF16),
            pltpu.VMEM((features, 2 * head_cols), BF16),
            pltpu.VMEM((n_mp, head_cols, part), BF16),
            pltpu.VMEM((rows, features), BF16),
            pltpu.VMEM((rows, head_cols), BF16),
            pltpu.VMEM((n_seq, rows, 2 * head_cols), BF16),
            pltpu.VMEM((n_mp, rows, head_cols), BF16),
            pltpu.SemaphoreType.REGULAR,
            pltpu.SemaphoreType.REGULAR,
            pltpu.SemaphoreType.DMA((2,)),
            pltpu.SemaphoreType.DMA((4,)),
            pltpu.SemaphoreType.DMA,
            pltpu.SemaphoreType.DMA((3, X_PIECES)),
            pltpu.SemaphoreType.DMA((3, X_PIECES)),
            pltpu.SemaphoreType.DMA((n_seq, 2)),
            pltpu.SemaphoreType.DMA((n_seq, 2)),
            pltpu.SemaphoreType.DMA((5,)),
            pltpu.SemaphoreType.DMA((5,)),
            pltpu.SemaphoreType.DMA((3, heads)),
            pltpu.SemaphoreType.DMA((3, heads)),
            pltpu.SemaphoreType.DMA((4, X_PIECES)),
            pltpu.SemaphoreType.DMA((4, X_PIECES)),
        ],
        compiler_params=pltpu.CompilerParams(
            collective_id=0, has_side_effects=True, vmem_limit_bytes=VMEM_BYTES
        ),
    )(softness, x, gain.reshape(1, features), wq, wk, wv, wo)


def solution(mesh):
    short = mesh.shape["mp"] == 4 and mesh.shape["seq"] == 4 and mesh.shape["groups"] == 2
    return jax.shard_map(
        functools.partial(line_call if short else per_device, mesh.shape["mp"], mesh.shape["seq"]),
        mesh=mesh,
        in_specs=(
            P(("groups", "seq"), "mp"),
            P(),
            P(None, "mp"),
            P(None, "mp"),
            P(None, "mp"),
            P("mp"),
            P("mp", None),
        ),
        out_specs=P(("groups", "seq"), "mp"),
        check_vma=False,
    )
```

```python
import functools
import math

import jax
import jax.numpy as jnp
from jax import lax
from jax.experimental import pallas as pl
from jax.experimental.pallas import tpu as pltpu
from jax.sharding import PartitionSpec as P

MESH = pl.DeviceIdType.MESH
F32 = jnp.float32
BF16 = jnp.bfloat16
UNROLL_LIMIT = 8
RS_PIECES = 2
X_PIECES = 2
VMEM_BYTES = 60 * 1024 * 1024


def remote(src, dst, send_sem, recv_sem, axis, index):
    return pltpu.make_async_remote_copy(
        src_ref=src,
        dst_ref=dst,
        send_sem=send_sem,
        recv_sem=recv_sem,
        device_id={axis: index},
        device_id_type=MESH,
    )


def each(count, body):
    if count <= UNROLL_LIMIT:
        for i in range(count):
            body(i)
    else:
        lax.fori_loop(0, count, lambda i, c: (body(i), c)[1], 0)


def kernel(
    n_mp,
    n_seq,
    softness_hbm,
    x_hbm,
    gain_hbm,
    wq_hbm,
    wk_hbm,
    wv_hbm,
    wo_hbm,
    out_ref,
    softness_ref,
    gain_ref,
    xg,
    wq,
    wk,
    wv,
    wo,
    normed,
    q_ref,
    kv,
    scores,
    heads,
    out_send,
    out_recv,
    small_sem,
    w_sem,
    x_sem,
    xg_send,
    xg_recv,
    kv_send,
    kv_recv,
    rs_send,
    rs_recv,
):
    me = lax.axis_index("mp")
    spot = lax.axis_index("seq")
    rows, part = x_hbm.shape
    head_cols = wq_hbm.shape[1]
    groups = softness_hbm.shape[0]
    span = head_cols // groups
    paired = n_mp == 4
    has_left = spot > 0
    has_right = spot < n_seq - 1
    hop = n_seq == 4
    ends = (spot == 0) | (spot == n_seq - 1)

    own_x = pltpu.make_async_copy(x_hbm, xg.at[me], x_sem)
    own_x.start()
    smalls = [
        pltpu.make_async_copy(gain_hbm, gain_ref, small_sem.at[0]),
        pltpu.make_async_copy(softness_hbm, softness_ref, small_sem.at[1]),
    ]
    for small in smalls:
        small.start()
    loads = [
        pltpu.make_async_copy(src, dst, w_sem.at[i])
        for i, (src, dst) in enumerate(((wk_hbm, wk), (wv_hbm, wv), (wq_hbm, wq), (wo_hbm, wo)))
    ]
    for load in loads:
        load.start()

    barrier = pltpu.get_barrier_semaphore()
    for step in range(1, n_mp):
        pl.semaphore_signal(
            barrier, inc=1, device_id={"mp": lax.rem(me + step, n_mp)}, device_id_type=MESH
        )

    @pl.when(has_left)
    def _():
        pl.semaphore_signal(barrier, inc=1, device_id={"seq": spot - 1}, device_id_type=MESH)

    @pl.when(has_right)
    def _():
        pl.semaphore_signal(barrier, inc=1, device_id={"seq": spot + 1}, device_id_type=MESH)

    greeted = n_mp - 1 + has_left.astype(jnp.int32) + has_right.astype(jnp.int32)
    if hop:

        @pl.when(ends)
        def _():
            pl.semaphore_signal(
                barrier, inc=1, device_id={"seq": n_seq - 1 - spot}, device_id_type=MESH
            )

        greeted = greeted + ends.astype(jnp.int32)
    pl.semaphore_wait(barrier, greeted)

    half = rows // 2
    pieces = [pl.ds(0, half), pl.ds(half, half)]
    near = me + 1 - 2 * lax.rem(me, 2)
    far = lax.rem(me + 2, n_mp)
    cross = lax.rem(near + 2, n_mp)
    sends = []

    def gather(lane, c, source, target):
        slot = xg.at[source, pieces[c]]
        return remote(slot, slot, xg_send.at[lane, c], xg_recv.at[lane, c], "mp", target)

    if paired:
        for lane, peer in ((0, far), (1, near)):
            for c, piece in enumerate(pieces):
                send = remote(
                    x_hbm.at[piece], xg.at[me, piece],
                    xg_send.at[lane, c], xg_recv.at[lane, c], "mp", peer,
                )
                send.start()
                sends.append(send)
    else:
        for c, piece in enumerate(pieces):
            for step in range(1, n_mp):
                send = remote(
                    x_hbm.at[piece], xg.at[me, piece],
                    xg_send.at[step, c], xg_recv.at[step, c], "mp", lax.rem(me + step, n_mp),
                )
                send.start()
                sends.append(send)
    own_x.wait()
    for small in smalls:
        small.wait()

    def relay_far(c):
        if paired:
            gather(0, c, far, far).wait_recv()
            relay = gather(2, c, far, near)
            relay.start()
            sends.append(relay)

    def gathered(c):
        if paired:
            gather(1, c, near, near).wait_recv()
            gather(2, c, cross, near).wait_recv()
        else:
            for step in range(1, n_mp):
                source = lax.rem(me - step + n_mp, n_mp)
                gather(step, c, source, source).wait_recv()

    features = n_mp * part

    def normalize(c):
        piece = pieces[c]
        total = jnp.zeros((half, 1), F32)
        for j in range(n_mp):
            total = total + jnp.sum(xg[j, piece, :].astype(F32), axis=-1, keepdims=True)
        average = total / features
        square = jnp.zeros((half, 1), F32)
        for j in range(n_mp):
            off = xg[j, piece, :].astype(F32) - average
            square = square + jnp.sum(off * off, axis=-1, keepdims=True)
        inverse = lax.rsqrt(square / features + 1e-05)
        for j in range(n_mp):
            cols = pl.ds(j * part, part)
            off = xg[j, piece, :].astype(F32) - average
            normed[piece, cols] = (off * inverse * gain_ref[:, cols]).astype(BF16)

    def block(way, which, owner, c, target):
        slot = kv.at[which, owner, pieces[c]]
        return remote(
            slot, slot, kv_send.at[way, which, owner, c], kv_recv.at[which, owner, c], "seq", target
        )

    def project(which, weight, c):
        kv[which, spot, pieces[c]] = jnp.dot(
            normed[pieces[c], :], weight[...], preferred_element_type=F32
        ).astype(BF16)
        launch(which, c)

    def launch(which, c):
        @pl.when(has_right)
        def _():
            block(1, which, spot, c, spot + 1).start()

        @pl.when(has_left)
        def _():
            block(0, which, spot, c, spot - 1).start()

        if hop:

            @pl.when(ends)
            def _():
                block(2, which, spot, c, n_seq - 1 - spot).start()

    relay_far(0)
    gathered(0)
    normalize(0)
    relay_far(1)
    loads[0].wait()
    project(0, wk, 0)
    gathered(1)
    normalize(1)
    project(0, wk, 1)
    loads[1].wait()
    kv[1, spot] = jnp.dot(normed[...], wv[...], preferred_element_type=F32).astype(BF16)
    for c in range(2):
        launch(1, c)
    loads[2].wait()
    q_ref[...] = jnp.dot(normed[...], wq[...], preferred_element_type=F32).astype(BF16)

    def take(which, step, c, forward):
        before = spot - step
        after = spot + step

        @pl.when(before >= 0)
        def _():
            block(1, which, before, c, before).wait_recv()
            if forward:

                @pl.when(has_right)
                def _():
                    block(1, which, before, c, spot + 1).start()

        @pl.when(after < n_seq)
        def _():
            block(0, which, after, c, after).wait_recv()
            if forward:

                @pl.when(has_left)
                def _():
                    block(0, which, after, c, spot - 1).start()

    if hop:
        for which in range(2):
            for c in range(2):
                take(which, 1, c, True)
        for step in (2, 3):
            for c in range(2):
                take(0, step, c, False)

        def last_values():
            for step in (2, 3):
                for c in range(2):
                    take(1, step, c, False)

    else:

        def chain(i):
            for c in range(2):
                for which in range(2):
                    take(which, i + 1, c, True)

        each(n_seq - 1, chain)

        def last_values():
            pass

    if n_seq <= UNROLL_LIMIT:
        sums, chances = [], []
        for h in range(groups):
            cols = pl.ds(h * span, span)
            keys = kv[0, :, :, cols].reshape(n_seq * rows, span)
            s = lax.dot_general(
                q_ref[:, cols], keys, (((1,), (1,)), ((), ())), preferred_element_type=F32
            ) * (softness_ref[h] / math.sqrt(span))
            top = jnp.max(s, axis=-1, keepdims=True)
            w = jnp.exp(s - top)
            sums.append(jnp.sum(w, axis=-1, keepdims=True))
            chances.append(w.astype(BF16))
        last_values()
        for h in range(groups):
            cols = pl.ds(h * span, span)
            values = kv[1, :, :, cols].reshape(n_seq * rows, span)
            mixed = jnp.dot(chances[h], values, preferred_element_type=F32)
            heads[:, cols] = (mixed / sums[h]).astype(BF16)
    else:
        for h in range(groups):
            cols = pl.ds(h * span, span)
            factor = softness_ref[h] / math.sqrt(span)

            def first(b, top):
                s = lax.dot_general(
                    q_ref[:, cols], kv[0, b, :, cols], (((1,), (1,)), ((), ())),
                    preferred_element_type=F32,
                ) * factor
                scores[b] = s
                return jnp.maximum(top, jnp.max(s, axis=-1, keepdims=True))

            top = lax.fori_loop(0, n_seq, first, jnp.full((rows, 1), -jnp.inf, F32))

            def second(b, state):
                summed, mixed = state
                w = jnp.exp(scores[b] - top)
                mixed = mixed + jnp.dot(
                    w.astype(BF16), kv[1, b, :, cols], preferred_element_type=F32
                )
                return summed + jnp.sum(w, axis=-1, keepdims=True), mixed

            summed, mixed = lax.fori_loop(
                0, n_seq, second, (jnp.zeros((rows, 1), F32), jnp.zeros((rows, span), F32))
            )
            heads[:, cols] = (mixed / summed).astype(BF16)

    loads[3].wait()
    rs_pieces = [pl.ds(i * (rows // RS_PIECES), rows // RS_PIECES) for i in range(RS_PIECES)]

    def share(owner):
        cols = pl.ds(pl.multiple_of(owner * part, part), part)
        return jnp.dot(heads[...], wo[:, cols], preferred_element_type=F32)

    if paired:
        quarter = rows // len(rs_pieces)

        def reduce(lane, piece, target):
            return remote(
                out_send.at[lane, piece], out_recv.at[lane, piece],
                rs_send.at[lane, piece.start // quarter], rs_recv.at[lane, piece.start // quarter],
                "mp", target,
            )

        out_send[0] = share(cross).astype(BF16)
        for piece in rs_pieces:
            send = reduce(0, piece, near)
            send.start()
            sends.append(send)
        for_far = share(far)
        for piece in rs_pieces:
            reduce(0, piece, near).wait_recv()
            low = piece.start
            out_send[2, piece] = (
                for_far[low : low + quarter] + out_recv[0, piece].astype(F32)
            ).astype(BF16)
            send = reduce(2, piece, far)
            send.start()
            sends.append(send)
        out_send[1] = share(near).astype(BF16)
        for piece in rs_pieces:
            send = reduce(1, piece, near)
            send.start()
            sends.append(send)
        own = share(me) + xg[me].astype(F32)
        for piece in rs_pieces:
            reduce(1, piece, near).wait_recv()
        own = own + out_recv[1].astype(F32)
        for piece in rs_pieces:
            reduce(2, piece, far).wait_recv()
            low = piece.start
            out_ref[piece, :] = (
                own[low : low + quarter] + out_recv[2, piece].astype(F32)
            ).astype(BF16)
    else:
        for step in range(1, n_mp):
            peer = lax.rem(me + step, n_mp)
            out_send[step] = share(peer).astype(BF16)
            send = remote(
                out_send.at[step], out_recv.at[step], rs_send.at[step, 0], rs_recv.at[step, 0], "mp", peer
            )
            send.start()
            sends.append(send)
        own = share(me) + xg[me].astype(F32)
        for step in range(1, n_mp):
            remote(
                out_send.at[step], out_recv.at[step], rs_send.at[step, 0], rs_recv.at[step, 0], "mp", me
            ).wait_recv()
            own = own + out_recv[step].astype(F32)
        out_ref[...] = own.astype(BF16)

    for send in sends:
        send.wait_send()

    def drain(b):
        for which in range(2):
            for c in range(2):
                to_right = (b == spot) | (b == spot - 1) if hop else b <= spot
                to_left = (b == spot) | (b == spot + 1) if hop else b >= spot

                @pl.when(has_right & to_right)
                def _():
                    block(1, which, b, c, spot + 1).wait_send()

                @pl.when(has_left & to_left)
                def _():
                    block(0, which, b, c, spot - 1).wait_send()

                if hop:

                    @pl.when(ends & (b == spot))
                    def _():
                        block(2, which, b, c, n_seq - 1 - spot).wait_send()

    each(n_seq, drain)


def per_device(n_mp, n_seq, x, gain, wq, wk, wv, softness, wo):
    rows, part = x.shape
    features, head_cols = wq.shape
    span_rows = n_seq if n_seq > UNROLL_LIMIT else 1
    any_space = pl.BlockSpec(memory_space=pl.ANY)
    vmem = pl.BlockSpec(memory_space=pltpu.VMEM)
    slots = max(n_mp, 3)
    return pl.pallas_call(
        functools.partial(kernel, n_mp, n_seq),
        out_shape=pltpu.VMEM((rows, part), BF16),
        in_specs=[
            any_space, any_space, any_space, any_space, any_space, any_space, any_space,
        ],
        out_specs=vmem,
        scratch_shapes=[
            pltpu.SMEM(softness.shape, F32),
            pltpu.VMEM((1, features), F32),
            pltpu.VMEM((n_mp, rows, part), BF16),
            pltpu.VMEM((features, head_cols), BF16),
            pltpu.VMEM((features, head_cols), BF16),
            pltpu.VMEM((features, head_cols), BF16),
            pltpu.VMEM((head_cols, features), BF16),
            pltpu.VMEM((rows, features), BF16),
            pltpu.VMEM((rows, head_cols), BF16),
            pltpu.VMEM((2, n_seq, rows, head_cols), BF16),
            pltpu.VMEM((span_rows, rows, rows), F32),
            pltpu.VMEM((rows, head_cols), BF16),
            pltpu.VMEM((slots, rows, part), BF16),
            pltpu.VMEM((slots, rows, part), BF16),
            pltpu.SemaphoreType.DMA((2,)),
            pltpu.SemaphoreType.DMA((4,)),
            pltpu.SemaphoreType.DMA,
            pltpu.SemaphoreType.DMA((slots, 2)),
            pltpu.SemaphoreType.DMA((slots, 2)),
            pltpu.SemaphoreType.DMA((3, 2, n_seq, 2)),
            pltpu.SemaphoreType.DMA((2, n_seq, 2)),
            pltpu.SemaphoreType.DMA((slots, RS_PIECES)),
            pltpu.SemaphoreType.DMA((slots, RS_PIECES)),
        ],
        compiler_params=pltpu.CompilerParams(collective_id=0, has_side_effects=True),
    )(softness, x, gain.reshape(1, features), wq, wk, wv, wo)


def line_kernel(
    softness_hbm, x_hbm, gain_hbm, wq_hbm, wk_hbm, wv_hbm, wo_hbm, out_ref,
    softness_ref, gain_ref, xg, xe, wq, wkv, wo, normed, q_ref, kv, heads,
    go_sem, up_sem, small_sem, w_sem, x_sem, xg_send, xg_recv, kv_send, kv_recv,
    wo_send, wo_recv, h_send, h_recv, e_send, e_recv,
):
    n_mp, n_seq = xg.shape[0], kv.shape[0]
    me = lax.axis_index("mp")
    spot = lax.axis_index("seq")
    group = lax.axis_index("groups")
    other = 1 - group
    rows, part = x_hbm.shape
    head_cols = wq_hbm.shape[1]
    groups = softness_hbm.shape[0]
    span = head_cols // groups
    features = n_mp * part
    last = n_seq - 1
    has_left = spot > 0
    has_right = spot < last
    is_first = spot == 0
    is_last = spot == last
    at_end = is_first | is_last
    opposite = last - spot
    odd = lax.rem(me, 2)
    is_odd = odd == 1
    is_even = odd == 0
    near = me + 1 - 2 * odd
    far = lax.rem(me + 2, n_mp)
    cross = lax.rem(near + 2, n_mp)
    even_me = me - odd
    odd_me = even_me + 1

    def columns(owner):
        return pl.ds(pl.multiple_of(owner * part, part), part)

    own_x = pltpu.make_async_copy(x_hbm, xg.at[me], x_sem)
    own_x.start()

    barrier = pltpu.get_barrier_semaphore()

    def greet(**where):
        pl.semaphore_signal(barrier, inc=1, device_id=where, device_id_type=MESH)

    leader = jnp.where(is_last, me, odd_me)

    @pl.when(is_odd | is_last)
    def _():
        greet(mp=far)

    @pl.when(is_even | is_last)
    def _():
        greet(mp=near)
        greet(mp=cross)

    greet(groups=other, mp=leader)
    for plane in range(n_seq):

        @pl.when(plane > spot)
        def _():
            greet(seq=plane, mp=me if plane == last else odd_me)

        @pl.when(plane < spot)
        def _():
            greet(seq=plane, mp=even_me)

    smalls = [
        pltpu.make_async_copy(gain_hbm, gain_ref, small_sem.at[0]),
        pltpu.make_async_copy(softness_hbm, softness_ref, small_sem.at[1]),
    ]
    for small in smalls:
        small.start()
    loads = [
        pltpu.make_async_copy(src, dst, w_sem.at[i])
        for i, (src, dst) in enumerate(
            (
                (wk_hbm, wkv.at[:, pl.ds(0, head_cols)]),
                (wv_hbm, wkv.at[:, pl.ds(head_cols, head_cols)]),
                (wq_hbm, wq),
                (wo_hbm.at[:, columns(me)], wo.at[me]),
            )
        )
    ]
    for load in loads:
        load.start()

    @pl.when(is_last)
    def _():
        pl.semaphore_wait(barrier, n_mp + spot)

    @pl.when(is_odd & has_right)
    def _():
        pl.semaphore_wait(barrier, n_mp - 1 + 2 + 2 * spot)
        pl.semaphore_signal(go_sem, inc=1, device_id={"mp": near}, device_id_type=MESH)

    @pl.when(is_even & has_right)
    def _():
        pl.semaphore_wait(go_sem, 1)

    piece_rows = rows // X_PIECES
    half = rows // 2
    halves = [pl.ds(0, half), pl.ds(half, half)]
    pieces = [pl.ds(c * piece_rows, piece_rows) for c in range(X_PIECES)]
    sends = []

    def gather(lane, c, source, target):
        slot = xg.at[source, pieces[c]]
        return remote(slot, slot, xg_send.at[lane, c], xg_recv.at[lane, c], "mp", target)

    for c, piece in enumerate(pieces):
        send = remote(
            x_hbm.at[piece], xg.at[me, piece],
            xg_send.at[0, c], xg_recv.at[0, c], "mp", far,
        )
        send.start()
        sends.append(send)
    def end_piece(lane, c, source, target, axis="mp"):
        slot = xe.at[source, pieces[c]]
        return remote(slot, slot, e_send.at[lane, c], e_recv.at[lane, c], axis, target)

    def to_other_end(c):
        return remote(
            x_hbm.at[pieces[c]], xe.at[me, pieces[c]],
            e_send.at[3, c], e_recv.at[3, c], "seq", opposite,
        )

    def send_to_other_end(when):
        @pl.when(when)
        def _():
            for c in range(X_PIECES):
                to_other_end(c).start()

    send_to_other_end(is_last)
    send = remote(x_hbm, xg.at[me], xg_send.at[1, 0], xg_recv.at[1, 0], "mp", near)
    send.start()
    sends.append(send)
    own_x.wait()
    for small in smalls:
        small.wait()

    def relay_far(c):
        gather(0, c, far, far).wait_recv()
        relay = gather(2, c, far, near)
        relay.start()
        sends.append(relay)

    def gathered(c):
        if c == 0:
            remote(
                x_hbm, xg.at[near], xg_send.at[1, 0], xg_recv.at[1, 0], "mp", near
            ).wait_recv()
        gather(2, c, cross, near).wait_recv()

    def normalize(c, held):
        piece = pieces[c]
        total = jnp.zeros((piece_rows, 1), F32)
        for j in range(n_mp):
            total = total + jnp.sum(held[j, piece, :].astype(F32), axis=-1, keepdims=True)
        average = total / features
        square = jnp.zeros((piece_rows, 1), F32)
        for j in range(n_mp):
            off = held[j, piece, :].astype(F32) - average
            square = square + jnp.sum(off * off, axis=-1, keepdims=True)
        inverse = lax.rsqrt(square / features + 1e-05)
        for j in range(n_mp):
            cols = pl.ds(j * part, part)
            off = held[j, piece, :].astype(F32) - average
            normed[piece, cols] = (off * inverse * gain_ref[:, cols]).astype(BF16)

    def know_later_planes(when):
        @pl.when(when & is_even)
        def _():
            pl.semaphore_wait(barrier, 2 * (last - spot))
            pl.semaphore_signal(up_sem, inc=1, device_id={"mp": near}, device_id_type=MESH)

        @pl.when(when & is_odd)
        def _():
            pl.semaphore_wait(up_sem, 1)

    def block(owner, c, target, lane=None):
        slot = kv.at[owner, halves[c]]
        lane = target if lane is None else lane
        return remote(slot, slot, kv_send.at[lane, c], kv_recv.at[owner, c], "seq", target)

    def project(c, owner):
        kv[owner, halves[c]] = jnp.dot(
            normed[halves[c], :], wkv[...], preferred_element_type=F32
        ).astype(BF16)

    def launch(target, c, when):
        @pl.when(when)
        def _():
            block(spot, c, target).start()

    exit_rows = head_cols // 2

    def exit_half(lane, source, rows_of, target, axis):
        there = pl.ds(pl.multiple_of(rows_of * exit_rows, exit_rows), exit_rows)
        slot = wo.at[source, there]
        return remote(slot, slot, wo_send.at[lane], wo_recv.at[lane], axis, target)

    near_exit = remote(
        wo_hbm.at[:, columns(near)], wo.at[me], wo_send.at[0], wo_recv.at[0], "mp", near
    )
    mine = pl.ds(pl.multiple_of(group * exit_rows, exit_rows), exit_rows)
    exits = [
        remote(
            wo_hbm.at[mine, columns(peer)], wo.at[me, mine],
            wo_send.at[lane], wo_recv.at[lane], "mp", peer,
        )
        for lane, peer in ((1, far), (2, cross))
    ] + [near_exit]

    for send in exits:
        send.start()
        sends.append(send)
    for c in range(X_PIECES):
        relay_far(c)
    know_later_planes(is_first)
    send_to_other_end(is_first)
    for c in range(X_PIECES):
        gathered(c)
        normalize(c, xg)
        done = (c + 1) * piece_rows
        if done == half:
            loads[0].wait()
            loads[1].wait()
            project(0, spot)
            launch(0, 0, spot == 1)
            launch(1, 0, spot == 2)
    project(1, spot)
    launch(0, 1, spot == 1)
    launch(1, 1, spot == 2)
    know_later_planes(has_left & has_right)
    for c in range(2):
        launch(last, c, spot == last - 1)
    for target in range(1, last):
        for c in range(2):
            launch(target, c, spot < target)
    for target in range(last - 1, 0, -1):
        for c in range(2):
            launch(target, c, spot == last)

    loads[2].wait()
    q_ref[...] = jnp.dot(normed[...], wq[...], preferred_element_type=F32).astype(BF16)

    def weigh(queries, keys, h):
        s = lax.dot_general(
            queries, keys, (((1,), (1,)), ((), ())), preferred_element_type=F32
        ) * (softness_ref[h] / math.sqrt(span))
        top = jnp.max(s, axis=-1, keepdims=True)
        w = jnp.exp(s - top)
        return jnp.sum(w, axis=-1, keepdims=True), w.astype(BF16)

    head = [pl.ds(h * span, span) for h in range(groups)]
    passes_up = spot == last - 1
    passes_down = spot == 1

    def exchanged(b):
        ends = (0, last)
        return (spot != b) & (spot != last - b) if b in ends else spot != b

    def take_blocks():
        for owner in range(n_seq):
            seen = passes_up if owner == last - 2 else passes_down if owner == 2 else False

            @pl.when(exchanged(owner) & jnp.logical_not(seen))
            def _():
                for c in range(2):
                    block(owner, c, owner).wait_recv()

    def pass_exit(lane, source):
        exit_half(lane, source, group, source, "mp").wait_recv()
        send = exit_half(lane + 2, source, group, other, "groups")
        send.start()
        sends.append(send)

    pass_exit(1, far)

    @pl.when(at_end)
    def _():
        for c in range(X_PIECES):
            to_other_end(c).wait_recv()
            end_piece(0, c, me, far).start()
            end_piece(1, c, me, near).start()


    pass_exit(2, cross)

    @pl.when(at_end)
    def _():
        for c in range(X_PIECES):
            end_piece(0, c, far, far).wait_recv()
            end_piece(2, c, far, near).start()


    @pl.when(passes_up)
    def _():
        for c in range(2):
            block(last - 2, c, last - 2).wait_recv()
            block(last - 2, c, last, last - 1).start()

    @pl.when(passes_down)
    def _():
        for c in range(2):
            block(2, c, 2).wait_recv()
            block(2, c, 0, 1).start()

    @pl.when(at_end)
    def _():
        for c in range(X_PIECES):
            end_piece(1, c, near, near).wait_recv()
            end_piece(2, c, cross, near).wait_recv()
            normalize(c, xe)
        kv[opposite] = jnp.dot(normed[...], wkv[...], preferred_element_type=F32).astype(BF16)

    def share(lane, h, source, target):
        slot = heads.at[source, :, head[h]]
        return remote(slot, slot, h_send.at[lane, h], h_recv.at[lane, h], "mp", target)

    def give(h, mixed):
        heads[me, :, head[h]] = mixed.astype(BF16)
        share(0, h, me, far).start()

    take_blocks()
    known = []
    for h in range(groups):
        keys = kv[:, :, head[h]].reshape(n_seq * rows, span)
        known.append(weigh(q_ref[:, head[h]], keys, h))
    for h in range(groups):
        values = kv[:, :, pl.ds(head_cols + h * span, span)].reshape(n_seq * rows, span)
        summed, w = known[h]
        give(h, jnp.dot(w, values, preferred_element_type=F32) / summed)

    gifts = []
    for h in range(groups):
        gifts += [share(0, h, me, far), share(1, h, me, cross)]
        send = share(2, h, me, near)
        send.start()
        gifts.append(send)

    @pl.when(is_even)
    def _():
        for h in range(groups):
            share(1, h, me, cross).start()

    loads[3].wait()
    total = xg[me].astype(F32) + jnp.dot(heads[me], wo[me], preferred_element_type=F32)
    for send in sends:
        send.wait_send()

    for target in range(n_seq):

        by_relay = spot == last - 2 if target == last else spot == 2 if target == 0 else False

        @pl.when(exchanged(target) & jnp.logical_not(by_relay))
        def _():
            for c in range(2):
                block(spot, c, target).wait_send()

    @pl.when(passes_up)
    def _():
        for c in range(2):
            block(last - 2, c, last, last - 1).wait_send()

    @pl.when(passes_down)
    def _():
        for c in range(2):
            block(2, c, 0, 1).wait_send()

    @pl.when(at_end)
    def _():
        for c in range(X_PIECES):
            to_other_end(c).wait_send()
            end_piece(0, c, me, far).wait_send()
            end_piece(1, c, me, near).wait_send()
            end_piece(2, c, far, near).wait_send()

    near_exit.wait_recv()
    for lane, source in ((1, far), (2, cross)):
        exit_half(lane + 2, source, other, other, "groups").wait_recv()
    for lane, source in ((2, near), (0, far), (1, cross)):
        for h in range(groups):
            share(lane, h, source, source).wait_recv()
            if lane == 0:

                @pl.when(is_odd)
                def _():
                    share(1, h, source, near).start()

        total = total + jnp.dot(heads[source], wo[source], preferred_element_type=F32)
    out_ref[...] = total.astype(BF16)

    for send in gifts:
        send.wait_send()


def line_call(n_mp, n_seq, x, gain, wq, wk, wv, softness, wo):
    rows, part = x.shape
    features, head_cols = wq.shape
    heads = softness.shape[0]
    any_space = pl.BlockSpec(memory_space=pl.ANY)
    return pl.pallas_call(
        line_kernel,
        out_shape=pltpu.VMEM((rows, part), BF16),
        in_specs=[any_space] * 7,
        out_specs=pl.BlockSpec(memory_space=pltpu.VMEM),
        scratch_shapes=[
            pltpu.SMEM(softness.shape, F32),
            pltpu.VMEM((1, features), F32),
            pltpu.VMEM((n_mp, rows, part), BF16),
            pltpu.VMEM((n_mp, rows, part), BF16),
            pltpu.VMEM((features, head_cols), BF16),
            pltpu.VMEM((features, 2 * head_cols), BF16),
            pltpu.VMEM((n_mp, head_cols, part), BF16),
            pltpu.VMEM((rows, features), BF16),
            pltpu.VMEM((rows, head_cols), BF16),
            pltpu.VMEM((n_seq, rows, 2 * head_cols), BF16),
            pltpu.VMEM((n_mp, rows, head_cols), BF16),
            pltpu.SemaphoreType.REGULAR,
            pltpu.SemaphoreType.REGULAR,
            pltpu.SemaphoreType.DMA((2,)),
            pltpu.SemaphoreType.DMA((4,)),
            pltpu.SemaphoreType.DMA,
            pltpu.SemaphoreType.DMA((3, X_PIECES)),
            pltpu.SemaphoreType.DMA((3, X_PIECES)),
            pltpu.SemaphoreType.DMA((n_seq, 2)),
            pltpu.SemaphoreType.DMA((n_seq, 2)),
            pltpu.SemaphoreType.DMA((5,)),
            pltpu.SemaphoreType.DMA((5,)),
            pltpu.SemaphoreType.DMA((3, heads)),
            pltpu.SemaphoreType.DMA((3, heads)),
            pltpu.SemaphoreType.DMA((4, X_PIECES)),
            pltpu.SemaphoreType.DMA((4, X_PIECES)),
        ],
        compiler_params=pltpu.CompilerParams(
            collective_id=0, has_side_effects=True, vmem_limit_bytes=VMEM_BYTES
        ),
    )(softness, x, gain.reshape(1, features), wq, wk, wv, wo)


def solution(mesh):
    short = mesh.shape["mp"] == 4 and mesh.shape["seq"] == 4 and mesh.shape["groups"] == 2
    return jax.shard_map(
        functools.partial(line_call if short else per_device, mesh.shape["mp"], mesh.shape["seq"]),
        mesh=mesh,
        in_specs=(
            P(("groups", "seq"), "mp"),
            P(),
            P(None, "mp"),
            P(None, "mp"),
            P(None, "mp"),
            P("mp"),
            P("mp", None),
        ),
        out_specs=P(("groups", "seq"), "mp"),
        check_vma=False,
    )
```
